32 devices in a mesh: dp: 8 (over z, x), tensor: 4 (over y, core).
Axes of the slice: x: 2, y: 2, z: 4, core: 2. Of those that a mesh axis runs over, the one named last changes fastest.
Arguments:
- tokens: bfloat16 [1024, 4096], P(('dp', 'tensor')), may hold values from -6 to 6
- cotangent: bfloat16 [1024, 4096], P(('dp', 'tensor')), may hold values from -6 to 6
- up_blocks: bfloat16 [8, 4, 32, 128, 128], P('dp', 'tensor'), may hold values from -0.25 to 0.25
- up_place: int32 [8, 4, 32], P('dp', 'tensor'), may hold values from -1 to 1023, as said below
- down_blocks: bfloat16 [8, 4, 32, 128, 128], P('dp', 'tensor'), may hold values from -0.125 to 0.125
- down_place: int32 [8, 4, 32], P('dp', 'tensor'), may hold values from -1 to 1023, as said below
Outputs:
- outputs: bfloat16 [1024, 4096], P(('dp', 'tensor'))
- input_grads: bfloat16 [1024, 4096], P(('dp', 'tensor'))
- up_grads: float32 [8, 4, 16, 128, 128], P('dp', 'tensor')
- down_grads: float32 [8, 4, 16, 128, 128], P('dp', 'tensor')
The draws below stay inside these ranges and needn't reach their ends.
Inputs may be any that keep to these rules, and one draw needn't show every extreme that they name: `up_place`: A code q = r * 32 + c names the up projection block at block r of the model width and block c of the tensor index's 32 hidden blocks; -1 marks an empty slot. On each device the live slots come first; the live codes of one tensor index are distinct and number exactly 128 over its devices; every tensor index has a device with 32 live slots and one with none. `down_place`: the same for the down projection: q = r * 32 + c names the block from hidden block c of the tensor index to block r of the model width; -1 marks an empty slot. Live slots come first on each device, live codes of one tensor index are distinct and number exactly 128, and every tensor index has a device with 32 live slots and one with none.
All inputs are finite; a program needn't handle non-finite values.
Results may differ from the reference program's by a relative error of at most 0.0095.
Values may be sent and summed in bfloat16 or wider, within the bound.
No kernel may reach another device: no remote copies, remote signals or barrier semaphores. Data moves between devices by JAX's collectives and lax.ppermute only.
A program may use at most 128 MiB of HBM per device.

```python
import math
import jax
import jax.numpy as jnp
from jax import lax

D = 4096
FF = 16384
BLK = 128
TOKENS = 1024
DB = 32
GBLK = 32
SLOTS = 32
MEAN = 16
LIVE = 128
N_DP = 8
N_TENSOR = 4


def group_places(group_key):
    key_pair, key_shift, key_cells, key_order = jax.random.split(group_key, 4)
    half_count = N_DP // 2
    pairing = jax.random.permutation(key_pair, N_DP).astype(jnp.int32)
    shifts = jax.random.randint(key_shift, (half_count,), -MEAN, MEAN + 1).astype(jnp.int32)
    shifts = shifts.at[0].set(MEAN)
    counts = jnp.zeros((N_DP,), jnp.int32)
    counts = counts.at[pairing[:half_count]].set(MEAN + shifts)
    counts = counts.at[pairing[half_count:]].set(MEAN - shifts)
    cell_total = DB * GBLK
    others = jax.random.permutation(key_cells, cell_total - 1).astype(jnp.int32)
    chosen = jnp.concatenate([jnp.full((1,), cell_total - 1, jnp.int32), others[:LIVE - 1]])
    chosen = jax.random.permutation(key_order, chosen).astype(jnp.int32)
    offsets = (jnp.cumsum(counts) - counts).astype(jnp.int32)
    slot_index = jnp.arange(SLOTS, dtype=jnp.int32)
    list_index = jnp.clip(offsets[:, None] + slot_index[None, :], 0, LIVE - 1)
    is_live = slot_index[None, :] < counts[:, None]
    block_codes = jnp.where(is_live, chosen[list_index], -1)
    return block_codes.astype(jnp.int32)


def all_places(base_key, salt):
    group_keys = jax.random.split(jax.random.fold_in(base_key, salt), N_TENSOR)
    grouped = jax.vmap(group_places)(group_keys)
    return jnp.transpose(grouped, (1, 0, 2)).astype(jnp.int32)


def draw_up_place(key, part):
    return all_places(key, 11)


def draw_down_place(key, part):
    return all_places(key, 23)


def level_of(rng, shape, cuts, smallest, largest):
    gain = 1.0
    for dim, shards_of in cuts:
        heights = jax.random.uniform(jax.random.fold_in(jax.random.fold_in(rng, 6), dim), (shards_of,), jnp.float32, smallest / len(cuts), largest / len(cuts))
        gain = gain * jnp.repeat(jnp.exp(heights), shape[dim] // shards_of).reshape((-1,) + (1,) * (len(shape) - 1 - dim))
    return gain


def bell_draw(own_key, shape, spread, limit, pieces=(), held_as=jnp.bfloat16):
    loudness = level_of(own_key, shape, pieces, -0.22, 0.18) if pieces else 1.0
    entries = jax.random.normal(own_key, shape, jnp.float32) * spread * loudness
    return jnp.minimum(jnp.maximum(entries, -limit), limit).astype(held_as)


def setup_inputs(seed: int = 0) -> dict:
    arg_keys = jax.random.split(jax.random.key(seed), 7)
    return {
        "tokens": bell_draw(arg_keys[0], (TOKENS, D), 1.0, 6.0, ((0, 32),)),
        "cotangent": bell_draw(arg_keys[1], (TOKENS, D), 1.0, 6.0, ((0, 32),)),
        "up_blocks": bell_draw(arg_keys[2], (N_DP, N_TENSOR, SLOTS, BLK, BLK), (D // 8) ** -0.5, 0.25, ((0, 8), (1, 4))),
        "up_place": draw_up_place(jax.random.fold_in(arg_keys[6], 71), 0),
        "down_blocks": bell_draw(arg_keys[4], (N_DP, N_TENSOR, SLOTS, BLK, BLK), (FF // 8) ** -0.5, 0.125, ((0, 8), (1, 4))),
        "down_place": draw_down_place(jax.random.fold_in(arg_keys[6], 71), 0),
    }


gelu_root = 0.7978845608028654
gelu_cubic = 0.044715

def gelu_value(values):
    return 0.5 * values * (1.0 + jnp.tanh(gelu_root * (values + gelu_cubic * values * values * values)))

def gelu_slope(values):
    inner_tanh = jnp.tanh(gelu_root * (values + gelu_cubic * values * values * values))
    return 0.5 * (1.0 + inner_tanh) + 0.5 * values * (1.0 - inner_tanh * inner_tanh) * gelu_root * (1.0 + 3.0 * gelu_cubic * values * values)

def split_codes(block_codes):
    is_live = block_codes >= 0
    safe_codes = jnp.where(is_live, block_codes, 0)
    return (safe_codes // GBLK, safe_codes % GBLK, is_live)

def pack_order(block_codes):
    is_live = (block_codes >= 0).astype(jnp.int32)
    live_rank = (jnp.cumsum(is_live) - is_live).astype(jnp.int32)
    live_total = block_codes.shape[0] // 2
    target = jnp.where(is_live > 0, live_rank, live_total).astype(jnp.int32)
    return jnp.zeros((live_total,), jnp.int32).at[target].set(block_codes.astype(jnp.int32), mode='drop')

def rounded(values):
    return lax.optimization_barrier(values.astype(jnp.bfloat16)).astype(jnp.float32)

def reference(tokens, cotangent, up_blocks, up_place, down_blocks, down_place):
    token_cube = tokens.reshape(TOKENS, DB, BLK).astype(jnp.float32)
    cotan_cube = cotangent.reshape(TOKENS, DB, BLK).astype(jnp.float32)
    grad_scale = 1.0 / math.sqrt(TOKENS)

    def per_group(totals, tensor_index):
        out_total, in_total = totals
        up_group = lax.dynamic_index_in_dim(up_blocks, tensor_index, 1, keepdims=False).reshape(N_DP * SLOTS, BLK, BLK).astype(jnp.float32)
        down_group = lax.dynamic_index_in_dim(down_blocks, tensor_index, 1, keepdims=False).reshape(N_DP * SLOTS, BLK, BLK).astype(jnp.float32)
        up_codes = lax.dynamic_index_in_dim(up_place, tensor_index, 1, keepdims=False).reshape(N_DP * SLOTS)
        down_codes = lax.dynamic_index_in_dim(down_place, tensor_index, 1, keepdims=False).reshape(N_DP * SLOTS)
        up_rows, up_cols, up_live = split_codes(up_codes)
        down_rows, down_cols, down_live = split_codes(down_codes)
        up_cols_drop = jnp.where(up_live, up_cols, GBLK)
        up_rows_drop = jnp.where(up_live, up_rows, DB)
        down_cols_drop = jnp.where(down_live, down_cols, GBLK)
        down_rows_drop = jnp.where(down_live, down_rows, DB)
        products = jnp.einsum('tsa,sab->tsb', jnp.take(token_cube, up_rows, axis=1), up_group)
        pre_act = jnp.zeros((TOKENS, GBLK, BLK), jnp.float32).at[:, up_cols_drop].add(products, mode='drop')
        hidden = gelu_value(pre_act).astype(jnp.bfloat16)
        hidden_wide = hidden.astype(jnp.float32)
        products = jnp.einsum('tsa,sab->tsb', jnp.take(hidden_wide, down_cols, axis=1), down_group)
        out_part = jnp.zeros((TOKENS, DB, BLK), jnp.float32).at[:, down_rows_drop].add(products, mode='drop')
        out_total = out_total + rounded(out_part)
        products = jnp.einsum('tsb,sab->tsa', jnp.take(cotan_cube, down_rows, axis=1), down_group)
        grad_hidden = jnp.zeros((TOKENS, GBLK, BLK), jnp.float32).at[:, down_cols_drop].add(products, mode='drop')
        grad_pre = (grad_hidden * gelu_slope(pre_act)).astype(jnp.bfloat16)
        grad_wide = grad_pre.astype(jnp.float32)
        products = jnp.einsum('tsb,sab->tsa', jnp.take(grad_wide, up_cols, axis=1), up_group)
        in_part = jnp.zeros((TOKENS, DB, BLK), jnp.float32).at[:, up_rows_drop].add(products, mode='drop')
        in_total = in_total + rounded(in_part)
        up_list = pack_order(up_codes)
        down_list = pack_order(down_codes)
        up_grad = jnp.einsum('tsa,tsb->sab', jnp.take(token_cube, up_list // GBLK, axis=1), jnp.take(grad_wide, up_list % GBLK, axis=1)) * grad_scale
        down_grad = jnp.einsum('tsa,tsb->sab', jnp.take(hidden_wide, down_list % GBLK, axis=1), jnp.take(cotan_cube, down_list // GBLK, axis=1)) * grad_scale
        return ((out_total, in_total), (up_grad.reshape(N_DP, MEAN, BLK, BLK), down_grad.reshape(N_DP, MEAN, BLK, BLK)))
    start_totals = (jnp.zeros((TOKENS, DB, BLK), jnp.float32), jnp.zeros((TOKENS, DB, BLK), jnp.float32))
    (out_total, in_total), (up_all, down_all) = lax.scan(per_group, start_totals, jnp.arange(N_TENSOR, dtype=jnp.int32))
    outputs = out_total.reshape(TOKENS, D).astype(jnp.bfloat16)
    input_grads = in_total.reshape(TOKENS, D).astype(jnp.bfloat16)
    up_grads = jnp.transpose(up_all, (1, 0, 2, 3, 4))
    down_grads = jnp.transpose(down_all, (1, 0, 2, 3, 4))
    return (outputs, input_grads, up_grads, down_grads)
```

```python
import functools
import math

import jax
import jax.numpy as jnp
from jax import lax
from jax.experimental import pallas as pl
from jax.experimental.pallas import tpu as pltpu
from jax.sharding import PartitionSpec as P

FF = 16384
BLK = 128
PACK = 16
VMEM_LIMIT = 40 << 20

gelu_root = 0.7978845608028654
gelu_cubic = 0.044715

SMEM_SPEC = pl.BlockSpec(memory_space=pltpu.SMEM)
VMEM_SPEC = pl.BlockSpec(memory_space=pltpu.VMEM)


def ring_order(devices):
    evens = list(range(0, devices, 2))
    odds = list(range(1, devices, 2))
    return evens + odds[::-1]


def ring_pairs(devices):
    order = ring_order(devices)
    ahead = [(order[i], order[(i + 1) % devices]) for i in range(devices)]
    behind = [(b, a) for a, b in ahead]
    return ahead, behind


def call(kernel, out_shape, in_specs, scratch=(), flops=0, nbytes=0, grid=None, out_specs=VMEM_SPEC):
    extra = {} if grid is None else {"grid": grid}
    return pl.pallas_call(
        kernel,
        out_shape=out_shape,
        in_specs=in_specs,
        out_specs=out_specs,
        scratch_shapes=list(scratch),
        compiler_params=pltpu.CompilerParams(vmem_limit_bytes=VMEM_LIMIT),
        cost_estimate=pl.CostEstimate(flops=flops, bytes_accessed=nbytes, transcendentals=0),
        **extra,
    )


def shape(dims, dtype):
    return jax.ShapeDtypeStruct(tuple(dims), dtype)


def dot(a, b, ca, cb):
    return lax.dot_general(a, b, (((ca,), (cb,)), ((), ())), preferred_element_type=jnp.float32)


def unroll_of(count):
    return math.gcd(count, 8)


def split_kernel(me_ref, x_ref, *outs):
    piece = outs[0].shape[1]
    for step, out in enumerate(outs):
        start = pl.multiple_of((me_ref[0] ^ step) * piece, piece)
        out[...] = x_ref[:, pl.ds(start, piece), :]


def split_blocks(me, blocks, devices):
    slots = blocks.shape[0]
    piece = BLK // devices
    out = [shape((slots, piece, BLK), blocks.dtype)] * devices
    return call(
        split_kernel, out, [SMEM_SPEC, VMEM_SPEC], out_specs=[VMEM_SPEC] * devices, nbytes=2 * blocks.size * 2
    )(me, blocks)


def pack_kernel(pick_ref, *refs):
    *ins, out_a, out_b, held = refs
    slots = ins[0].shape[0]
    half = out_a.shape[0]
    for step, part in enumerate(ins):
        held[step * slots : (step + 1) * slots] = part[...]
    unroll = unroll_of(half)

    def body(i, carry):
        for u in range(unroll):
            k = i * unroll + u
            out_a[k] = held[pick_ref[k]]
            out_b[k] = held[pick_ref[half + k]]
        return carry

    lax.fori_loop(0, half // unroll, body, 0)


def pack_pieces(pick, parts, live):
    slots, piece, _ = parts[0].shape
    out = [shape((live // 2, piece, BLK), parts[0].dtype)] * 2
    return call(
        pack_kernel,
        out,
        [SMEM_SPEC] + [VMEM_SPEC] * len(parts),
        out_specs=[VMEM_SPEC] * 2,
        scratch=[pltpu.VMEM((len(parts) * slots, piece, BLK), parts[0].dtype)],
        nbytes=3 * len(parts) * slots * piece * BLK,
    )(pick, *parts)


def join_kernel(ahead_ref, behind_ref, *refs):
    *ins, out = refs
    devices = len(ins) // 2
    half, piece, _ = ins[0].shape
    for j in range(devices):
        start = pl.multiple_of(ahead_ref[j] * piece, piece)
        out[:half, pl.ds(start, piece), :] = ins[j][...]
        start = pl.multiple_of(behind_ref[j] * piece, piece)
        out[half:, pl.ds(start, piece), :] = ins[devices + j][...]


def join_pieces(ahead, behind, first, second):
    half = first[0].shape[0]
    return call(
        join_kernel,
        shape((2 * half, BLK, BLK), first[0].dtype),
        [SMEM_SPEC] * 2 + [VMEM_SPEC] * (2 * len(first)),
        nbytes=8 * half * BLK * BLK,
    )(ahead, behind, *first, *second)


def lanes(ref, block):
    return ref[:, pl.ds(pl.multiple_of(block * BLK, BLK), BLK)]


def sum_blocks(acc, live, target, term):
    acc[...] = jnp.zeros_like(acc)
    unroll = unroll_of(live)

    def body(i, carry):
        products = [term(i * unroll + u) for u in range(unroll)]
        for u in range(unroll):
            acc[target(i * unroll + u)] += products[u]
        return carry

    lax.fori_loop(0, live // unroll, body, 0)


def hidden_kernel(rows_ref, cols_ref, tok_ref, w_ref, hid_ref, turned_ref, slope_ref, acc):
    sum_blocks(
        acc,
        w_ref.shape[0],
        lambda k: cols_ref[k],
        lambda k: dot(lanes(tok_ref, rows_ref[k]), w_ref[k], 1, 0),
    )

    def body(c, carry):
        values = acc[c]
        tanh = jnp.tanh(gelu_root * (values + gelu_cubic * values * values * values))
        hidden = 0.5 * values * (1.0 + tanh)
        hid_ref[c] = hidden.astype(jnp.bfloat16)
        turned_ref[c] = hidden.T.astype(jnp.bfloat16)
        slope_ref[c] = 0.5 * (1.0 + tanh) + 0.5 * values * (1.0 - tanh * tanh) * gelu_root * (
            1.0 + 3.0 * gelu_cubic * values * values
        )
        return carry

    lax.fori_loop(0, acc.shape[0], body, 0)


def grad_pre_kernel(rows_ref, cols_ref, cot_ref, w_ref, slope_ref, out_ref, acc):
    sum_blocks(
        acc,
        w_ref.shape[0],
        lambda k: cols_ref[k],
        lambda k: dot(lanes(cot_ref, rows_ref[k]), w_ref[k], 1, 1),
    )

    def body(c, carry):
        out_ref[c] = (acc[c] * slope_ref[c]).astype(jnp.bfloat16)
        return carry

    lax.fori_loop(0, acc.shape[0], body, 0)


def width_kernel(contract, rows_ref, cols_ref, x_ref, w_ref, out_ref, acc):
    sum_blocks(
        acc,
        w_ref.shape[0],
        lambda k: rows_ref[k],
        lambda k: dot(x_ref[cols_ref[k]], w_ref[k], 1, contract),
    )
    for r in range(acc.shape[0]):
        out_ref[:, r * BLK : (r + 1) * BLK] = acc[r].astype(jnp.bfloat16)


def up_terms_kernel(owner_ref, rows_ref, cols_ref, turned_ref, grad_ref, out_ref):
    mean = out_ref.shape[1]
    base = owner_ref[pl.program_id(0)] * mean
    for j in range(mean):
        start = pl.multiple_of(rows_ref[base + j] * BLK, BLK)
        out_ref[0, j] = dot(turned_ref[pl.ds(start, BLK), :], grad_ref[cols_ref[base + j]], 1, 0)


def down_terms_kernel(owner_ref, rows_ref, cols_ref, turned_ref, cot_ref, out_ref):
    mean = out_ref.shape[1]
    base = owner_ref[pl.program_id(0)] * mean
    for j in range(mean):
        out_ref[0, j] = dot(turned_ref[cols_ref[base + j]], lanes(cot_ref, rows_ref[base + j]), 1, 0)


def terms(kernel, owner, rows, cols, left, right):
    devices = owner.shape[0]
    live = rows.shape[0]
    mean = live // devices
    return call(
        kernel,
        shape((devices, mean, BLK, BLK), jnp.float32),
        [SMEM_SPEC] * 3 + [VMEM_SPEC] * 2,
        grid=(devices,),
        out_specs=pl.BlockSpec((1, mean, BLK, BLK), lambda i: (i, 0, 0, 0)),
        flops=2 * live * BLK**3 * 4,
        nbytes=live * BLK * BLK * 4 + 2 * (left.size + right.size),
    )(owner, rows, cols, left, right)


def ring_sum(parts, ahead, behind):
    devices = parts.shape[0]
    half = BLK // 2

    def low(q):
        return parts[q, :, :half]

    def high(q):
        return parts[q, :, half:]

    run_a = low(0)
    run_b = high((devices - 2) % devices)
    for step in range(1, devices):
        run_a = lax.ppermute(run_a.astype(jnp.bfloat16), "dp", ahead)
        run_b = lax.ppermute(run_b.astype(jnp.bfloat16), "dp", behind)
        last = step == devices - 1
        run_a = run_a.astype(jnp.float32) + low(step)
        run_b = run_b.astype(jnp.float32) + high(step if last else devices - 2 - step)
    return jnp.concatenate([run_a, run_b], axis=1)


def shards(tokens, cotangent, up_blocks, up_place, down_blocks, down_place):
    devices = lax.axis_size("dp")
    me = lax.axis_index("dp")
    slots = up_place.shape[2]
    mean = slots // 2
    live = devices * mean
    group_blocks = FF // BLK // lax.axis_size("tensor")
    model_width = tokens.shape[1]
    model_blocks = model_width // BLK

    order = ring_order(devices)
    place = {d: i for i, d in enumerate(order)}
    ahead, behind = ring_pairs(devices)
    nav = jnp.array(
        [
            [
                [order[(place[d] - j) % devices] for j in range(devices)],
                [order[(place[d] + j) % devices] for j in range(devices)],
                [order[(place[d] - 1 - j) % devices] for j in range(devices)],
            ]
            for d in range(devices)
        ],
        jnp.int32,
    )[me]
    from_ahead, from_behind, owner = nav[0], nav[1], nav[2]

    codes = lax.all_gather(
        jnp.stack([up_place.reshape(slots), down_place.reshape(slots)])[None], "dp", axis=0, tiled=True
    )
    codes = jnp.transpose(codes, (1, 0, 2))
    counts = jnp.sum((codes >= 0).astype(jnp.int32), axis=2)
    index = jnp.arange(devices, dtype=jnp.int32)
    ends = jnp.sum(jnp.where(index[None, None, :] <= index[None, :, None], counts[:, None, :], 0), axis=2)
    listed = jnp.arange(live, dtype=jnp.int32)
    holder = jnp.sum((listed[None, :, None] >= ends[:, None, :]).astype(jnp.int32), axis=2)
    offset = jnp.sum(jnp.where(index[None, None, :] < holder[:, :, None], counts[:, None, :], 0), axis=2)
    slot = listed[None, :] - offset
    source = holder * slots + slot
    every = jnp.arange(devices * slots, dtype=jnp.int32)
    flat = codes.reshape(2, devices * slots)
    code = jnp.sum(jnp.where(every[None, None, :] == source[:, :, None], flat[:, None, :], 0), axis=2)
    rows = code // group_blocks
    cols = code % group_blocks
    pick = (holder ^ me) * slots + slot

    tok = lax.all_gather(tokens, "tensor", axis=0, tiled=True)
    cot = lax.all_gather(cotangent, "tensor", axis=0, tiled=True)
    row_count = tok.shape[0]

    if BLK % (PACK * devices) == 0:
        here = me.reshape(1).astype(jnp.int32)

        def spread(blocks):
            parts = split_blocks(here, blocks.reshape(slots, BLK, BLK), devices)
            return [parts[0]] + [
                lax.ppermute(parts[s], "dp", [(i, i ^ s) for i in range(devices)]) for s in range(1, devices)
            ]

        def gather(parts, which):
            a, b = pack_pieces(pick[which], parts, live)
            first, second = [a], [b]
            for _ in range(1, devices):
                a, b = lax.ppermute(a, "dp", ahead), lax.ppermute(b, "dp", behind)
                first.append(a)
                second.append(b)
            return join_pieces(from_ahead, from_behind, first, second)

        up_parts = spread(up_blocks)
        down_parts = spread(down_blocks)
        up = gather(up_parts, 0)
        down = gather(down_parts, 1)
    else:

        def gather_all(blocks, which):
            every_slot = lax.all_gather(blocks.reshape(slots, BLK, BLK), "dp", axis=0, tiled=True)
            return jnp.take(every_slot, source[which], axis=0)

        up = gather_all(up_blocks, 0)
        down = gather_all(down_blocks, 1)

    flops = 2 * live * row_count * BLK * BLK * 4
    block_bytes = live * BLK * BLK * 2
    side = row_count * BLK
    group_acc = pltpu.VMEM((group_blocks, row_count, BLK), jnp.float32)
    model_acc = pltpu.VMEM((model_blocks, row_count, BLK), jnp.float32)
    tables = [SMEM_SPEC] * 2

    hid, hid_turned, slope = call(
        hidden_kernel,
        [
            shape((group_blocks, row_count, BLK), jnp.bfloat16),
            shape((group_blocks, BLK, row_count), jnp.bfloat16),
            shape((group_blocks, row_count, BLK), jnp.float32),
        ],
        tables + [VMEM_SPEC] * 2,
        out_specs=[VMEM_SPEC] * 3,
        scratch=[group_acc],
        flops=flops,
        nbytes=block_bytes + side * (2 * model_blocks + 8 * group_blocks),
    )(rows[0], cols[0], tok, up)

    down_terms = terms(down_terms_kernel, owner, rows[1], cols[1], hid_turned, cot)

    grad_pre = call(
        grad_pre_kernel,
        shape((group_blocks, row_count, BLK), jnp.bfloat16),
        tables + [VMEM_SPEC] * 3,
        scratch=[group_acc],
        flops=flops,
        nbytes=block_bytes + side * (2 * model_blocks + 6 * group_blocks),
    )(rows[1], cols[1], cot, down, slope)

    up_terms = terms(up_terms_kernel, owner, rows[0], cols[0], tok.T, grad_pre)

    def width(contract, which, x, w):
        return call(
            functools.partial(width_kernel, contract),
            shape((row_count, model_width), jnp.bfloat16),
            tables + [VMEM_SPEC] * 2,
            scratch=[model_acc],
            flops=flops,
            nbytes=block_bytes + side * (2 * model_blocks + 2 * group_blocks),
        )(rows[which], cols[which], x, w)

    out_part = width(0, 1, hid, down)
    in_part = width(1, 0, grad_pre, up)

    outputs = lax.psum_scatter(out_part, "tensor", scatter_dimension=0, tiled=True)
    input_grads = lax.psum_scatter(in_part, "tensor", scatter_dimension=0, tiled=True)

    scale = 1.0 / math.sqrt(devices * row_count)
    down_grads = ring_sum(down_terms, ahead, behind) * scale
    up_grads = ring_sum(up_terms, ahead, behind) * scale
    grads_shape = (1, 1, mean, BLK, BLK)
    return (outputs, input_grads, up_grads.reshape(grads_shape), down_grads.reshape(grads_shape))


def solution(mesh):
    return jax.shard_map(
        shards,
        mesh=mesh,
        in_specs=(
            P(("dp", "tensor"), None),
            P(("dp", "tensor"), None),
            P("dp", "tensor", None, None, None),
            P("dp", "tensor", None),
            P("dp", "tensor", None, None, None),
            P("dp", "tensor", None),
        ),
        out_specs=(
            P(("dp", "tensor"), None),
            P(("dp", "tensor"), None),
            P("dp", "tensor", None, None, None),
            P("dp", "tensor", None, None, None),
        ),
        check_vma=False,
    )
```

```python
import functools
import math

import jax
import jax.numpy as jnp
from jax import lax
from jax.experimental import pallas as pl
from jax.experimental.pallas import tpu as pltpu
from jax.sharding import PartitionSpec as P

FF = 16384
BLK = 128
PACK = 16
VMEM_LIMIT = 56 << 20

gelu_root = 0.7978845608028654
gelu_cubic = 0.044715

SMEM_SPEC = pl.BlockSpec(memory_space=pltpu.SMEM)
ANY_SPEC = pl.BlockSpec(memory_space=pl.ANY)


def ring_order(devices):
    evens = list(range(0, devices, 2))
    odds = list(range(1, devices, 2))
    return evens + odds[::-1]


def ring_pairs(devices):
    order = ring_order(devices)
    ahead = [(order[i], order[(i + 1) % devices]) for i in range(devices)]
    behind = [(b, a) for a, b in ahead]
    return ahead, behind


def shape(dims, dtype):
    return jax.ShapeDtypeStruct(tuple(dims), dtype)


def dot(a, b, ca, cb):
    return lax.dot_general(a, b, (((ca,), (cb,)), ((), ())), preferred_element_type=jnp.float32)


def unroll_of(count):
    return math.gcd(count, 8)


class Whole:
    sides = 1

    def __init__(self, array):
        self.arrays, self.tables = [array], []
        self.held = pltpu.VMEM(array.shape, array.dtype)

    def copies(self, tables, refs, held, sems):
        return [pltpu.make_async_copy(refs[0], held, sems.at[0])]


class Parts:
    def __init__(self, arrays, slots):
        self.arrays, self.tables, self.slots = list(arrays), [], slots
        first = arrays[0]
        self.held = pltpu.VMEM((len(arrays) * slots, *first.shape[1:]), first.dtype)

    def copies(self, tables, refs, held, sems):
        slots = self.slots
        return [
            pltpu.make_async_copy(ref.at[pl.ds(0, slots)], held.at[pl.ds(i * slots, slots)], sems.at[i])
            for i, ref in enumerate(refs)
        ]


class Joined:
    sides = 2

    def __init__(self, first, second, tables):
        self.arrays, self.tables = [*first, *second], list(tables)
        half = first[0].shape[0]
        self.held = pltpu.VMEM((2 * half, BLK, BLK), first[0].dtype)

    def copies(self, tables, refs, held, sems):
        half, piece, _ = refs[0].shape
        out = []
        for i, ref in enumerate(refs):
            side, j = divmod(i, len(refs) // 2)
            start = pl.multiple_of(tables[side][j] * piece, piece)
            to = held.at[pl.ds(side * half, half), pl.ds(start, piece), :]
            out.append(pltpu.make_async_copy(ref, to, sems.at[i]))
        return out


def run(kernel, small, items, outs, scratch=(), flops=0, nbytes=0, chunks=None):
    tables = [t for item in items for t in item.tables]
    arrays = [x for item in items for x in item.arrays]
    chunks = chunks or [0] * len(outs)

    def body(*refs):
        refs = list(refs)

        def take(n):
            taken = refs[:n]
            del refs[:n]
            return taken

        small_refs = take(len(small))
        table_refs = [take(len(item.tables)) for item in items]
        array_refs = [take(len(item.arrays)) for item in items]
        out_refs = take(len(outs))
        held_refs = take(len(items))
        result_refs = take(len(outs))
        scratch_refs = take(len(scratch))
        in_sems, out_sems = refs[: len(items)], refs[len(items) :]
        fetches = [
            item.copies(t, x, held, sems)
            for item, t, x, held, sems in zip(items, table_refs, array_refs, held_refs, in_sems, strict=True)
        ]
        for copies in fetches:
            for copy in copies:
                copy.start()

        def need(*which, part=(0, 1)):
            for i in which:
                size = len(fetches[i]) // part[1]
                for copy in fetches[i][part[0] * size : (part[0] + 1) * size]:
                    copy.wait()

        sent = {}

        def send(i, q=None):
            result, out, sem = result_refs[i], out_refs[i], out_sems[i].at[q or 0]
            if q is not None:
                result, out = result.at[q], out.at[q]
            sent[i, q] = pltpu.make_async_copy(result, out, sem)
            sent[i, q].start()

        kernel(need, send, *small_refs, *held_refs, *result_refs, *scratch_refs)
        for i, count in enumerate(chunks):
            for q in range(count) if count else [None]:
                if (i, q) not in sent:
                    send(i, q)
        for copy in sent.values():
            copy.wait()

    return pl.pallas_call(
        body,
        out_shape=list(outs),
        in_specs=[SMEM_SPEC] * (len(small) + len(tables)) + [ANY_SPEC] * len(arrays),
        out_specs=[ANY_SPEC] * len(outs),
        scratch_shapes=[
            *(item.held for item in items),
            *(pltpu.VMEM(x.shape, x.dtype) for x in outs),
            *scratch,
            *(pltpu.SemaphoreType.DMA((len(item.arrays),)) for item in items),
            *(pltpu.SemaphoreType.DMA((max(1, count),)) for count in chunks),
        ],
        compiler_params=pltpu.CompilerParams(vmem_limit_bytes=VMEM_LIMIT),
        cost_estimate=pl.CostEstimate(flops=flops, bytes_accessed=nbytes, transcendentals=0),
    )(*small, *tables, *arrays)


def split_blocks(me, up, down, note, devices):
    slots = up.shape[0]
    piece = BLK // devices

    def kernel(need, send, me_ref, up_ref, down_ref, note_ref, *outs):
        need(0, 1, 2)
        for step, out in enumerate(outs):
            start = pl.multiple_of((me_ref[0] ^ step) * piece, piece)
            out[:slots] = up_ref[:, pl.ds(start, piece), :]
            out[slots : 2 * slots] = down_ref[:, pl.ds(start, piece), :]
            out[2 * slots] = note_ref[...]
            send(step)

    out = [shape((2 * slots + 1, piece, BLK), up.dtype)] * devices
    return run(kernel, [me], [Whole(up), Whole(down), Whole(note)], out, nbytes=8 * up.size)


def pack_pieces(pick, parts, slots, live):
    piece = parts[0].shape[1]
    half = live // 2
    unroll = unroll_of(half)

    def kernel(need, send, up_pick, down_pick, held, *outs):
        need(0)
        for which, picked in enumerate((up_pick, down_pick)):
            ahead, behind = outs[2 * which : 2 * which + 2]

            def body(i, carry, picked=picked, ahead=ahead, behind=behind):
                for u in range(unroll):
                    k = i * unroll + u
                    ahead[k] = held[picked[k]]
                    behind[k] = held[picked[half + k]]
                return carry

            lax.fori_loop(0, half // unroll, body, 0)
            send(2 * which)
            send(2 * which + 1)

    out = [shape((half, piece, BLK), parts[0].dtype)] * 4
    items = [Parts(parts, 2 * slots)]
    return run(kernel, [pick[0], pick[1]], items, out, nbytes=6 * len(parts) * slots * piece * BLK)


def lanes(ref, block):
    return ref[:, pl.ds(pl.multiple_of(block * BLK, BLK), BLK)]


def sum_blocks(acc, live, sides, target, term, fetch):
    acc[...] = jnp.zeros_like(acc)
    count = live // sides
    unroll = unroll_of(count)
    for side in range(sides):
        fetch(side)

        def body(i, carry, first=side * count):
            products = [term(first + i * unroll + u) for u in range(unroll)]
            for u in range(unroll):
                acc[target(first + i * unroll + u)] += products[u]
            return carry

        lax.fori_loop(0, count // unroll, body, 0)


def fetch_of(need, item, sides):
    return lambda side: need(item, part=(side, sides))


def down_terms(owner_ref, rows_ref, cols_ref, turned_ref, cot_ref, out_ref, send):
    devices, mean = out_ref.shape[:2]
    for q in range(devices):
        base = owner_ref[q] * mean
        for j in range(mean):
            row, col = rows_ref[base + j], cols_ref[base + j]
            out_ref[q, j] = dot(turned_ref[col], lanes(cot_ref, row), 1, 0).astype(jnp.bfloat16)
        send(q)


def up_terms(owner_ref, rows_ref, cols_ref, turned_ref, grad_ref, out_ref, send):
    devices, mean = out_ref.shape[:2]
    for q in range(devices):
        base = owner_ref[q] * mean
        for j in range(mean):
            row, col = rows_ref[base + j], cols_ref[base + j]
            turned = turned_ref[pl.ds(pl.multiple_of(row * BLK, BLK), BLK), :]
            out_ref[q, j] = dot(turned, grad_ref[col], 1, 0).astype(jnp.bfloat16)
        send(q)


def hidden_kernel(sides, need, send, owner, rows, cols, down_rows, down_cols, tok, w, cot, hid, slope, out, acc, turned):
    need(0)
    fetch = fetch_of(need, 1, sides)
    sum_blocks(acc, w.shape[0], sides, lambda k: cols[k], lambda k: dot(lanes(tok, rows[k]), w[k], 1, 0), fetch)

    def body(c, carry):
        values = acc[c]
        tanh = jnp.tanh(gelu_root * (values + gelu_cubic * values * values * values))
        hidden = 0.5 * values * (1.0 + tanh)
        hid[c] = hidden.astype(jnp.bfloat16)
        turned[c] = hidden.T.astype(jnp.bfloat16)
        slope[c] = 0.5 * (1.0 + tanh) + 0.5 * values * (1.0 - tanh * tanh) * gelu_root * (
            1.0 + 3.0 * gelu_cubic * values * values
        )
        return carry

    lax.fori_loop(0, acc.shape[0], body, 0)
    send(0)
    send(1)
    need(2)
    down_terms(owner, down_rows, down_cols, turned, cot, out, lambda q: send(2, q))


def grad_pre_kernel(sides, need, send, owner, rows, cols, up_rows, up_cols, cot, w, slope, tok_turned, grad, out, acc):
    need(0)
    fetch = fetch_of(need, 1, sides)
    sum_blocks(acc, w.shape[0], sides, lambda k: cols[k], lambda k: dot(lanes(cot, rows[k]), w[k], 1, 1), fetch)
    need(2)

    def body(c, carry):
        grad[c] = (acc[c] * slope[c]).astype(jnp.bfloat16)
        return carry

    lax.fori_loop(0, acc.shape[0], body, 0)
    send(0)
    need(3)
    up_terms(owner, up_rows, up_cols, tok_turned, grad, out, lambda q: send(1, q))


def width_kernel(contract, sides, need, send, rows, cols, x, w, out, acc):
    need(0)
    fetch = fetch_of(need, 1, sides)
    sum_blocks(acc, w.shape[0], sides, lambda k: rows[k], lambda k: dot(x[cols[k]], w[k], 1, contract), fetch)
    for r in range(acc.shape[0]):
        out[:, r * BLK : (r + 1) * BLK] = acc[r].astype(jnp.bfloat16)


def tie(value, *others):
    return lax.optimization_barrier((value, others))[0]


class RingSum:
    def __init__(self, parts, ahead, behind):
        self.parts, self.ahead, self.behind = parts, ahead, behind
        self.devices = parts.shape[0]
        self.done = 0
        self.run = (self.low(0), self.high((self.devices - 2) % self.devices))

    def low(self, q):
        return self.parts[q, :, : BLK // 2]

    def high(self, q):
        return self.parts[q, :, BLK // 2 :]

    def step(self, *after):
        self.done += 1
        last = self.done == self.devices - 1
        a, b = (x.astype(jnp.bfloat16) for x in self.run)
        if after:
            a, b = tie((a, b), *after)
        a = lax.ppermute(a, "dp", self.ahead)
        b = lax.ppermute(b, "dp", self.behind)
        a = a.astype(jnp.float32) + self.low(self.done).astype(jnp.float32)
        q = self.done if last else self.devices - 2 - self.done
        b = b.astype(jnp.float32) + self.high(q).astype(jnp.float32)
        if not last:
            a, b = a.astype(jnp.bfloat16), b.astype(jnp.bfloat16)
        self.run = (a, b)
        return self.run

    def steps_left(self):
        return self.devices - 1 - self.done

    def total(self):
        return jnp.concatenate(self.run, axis=1)


def tables(rows, cols, owners):
    _, devices, slots = rows.shape
    live = devices * (slots // 2)
    counts = jnp.sum((cols >= 0).astype(jnp.int32), axis=2)
    earlier = owners[None, :] < owners[:, None]
    offset = jnp.sum(jnp.where(earlier[None], counts[:, None, :], 0), axis=2)
    within = jnp.arange(live, dtype=jnp.int32)[None, :, None] - offset[:, None, :]
    held = (within >= 0) & (within < counts[:, None, :])
    base = jnp.arange(devices, dtype=jnp.int32) * slots
    pick = jnp.sum(jnp.where(held, within + base[None, None, :], 0), axis=2)
    every = jnp.arange(devices * slots, dtype=jnp.int32)
    chosen = every[None, None, :] == pick[:, :, None]
    at = [jnp.sum(jnp.where(chosen, x.reshape(2, 1, devices * slots), 0), axis=2) for x in (rows, cols)]
    return pick, at[0], at[1]


def shards(tokens, cotangent, up_blocks, up_place, down_blocks, down_place):
    devices = lax.axis_size("dp")
    me = lax.axis_index("dp")
    slots = up_place.shape[2]
    mean = slots // 2
    live = devices * mean
    group_blocks = FF // BLK // lax.axis_size("tensor")
    row_count = tokens.shape[0] * lax.axis_size("tensor")
    model_width = tokens.shape[1]
    model_blocks = model_width // BLK

    order = ring_order(devices)
    place = {d: i for i, d in enumerate(order)}
    ahead, behind = ring_pairs(devices)
    nav = jnp.array(
        [
            [
                [order[(place[d] - j) % devices] for j in range(devices)],
                [order[(place[d] + j) % devices] for j in range(devices)],
                [order[(place[d] - 1 - j) % devices] for j in range(devices)],
            ]
            for d in range(devices)
        ],
        jnp.int32,
    )[me]
    from_ahead, from_behind, owner = nav[0], nav[1], nav[2]
    index = jnp.arange(devices, dtype=jnp.int32)
    up_slots = up_blocks.reshape(slots, BLK, BLK)
    down_slots = down_blocks.reshape(slots, BLK, BLK)
    codes = jnp.stack([up_place.reshape(1, slots), down_place.reshape(1, slots)])

    flops = 2 * live * row_count * BLK * BLK * 4
    block_bytes = live * BLK * BLK * 2
    side = row_count * BLK
    group_acc = pltpu.VMEM((group_blocks, row_count, BLK), jnp.float32)
    model_acc = pltpu.VMEM((model_blocks, row_count, BLK), jnp.float32)

    group_cube = (group_blocks, row_count, BLK)
    terms_shape = shape((devices, mean, BLK, BLK), jnp.bfloat16)

    def hidden_of(rows, cols, tok, cot, up):
        outs = [shape(group_cube, jnp.bfloat16), shape(group_cube, jnp.float32), terms_shape]
        return run(
            functools.partial(hidden_kernel, up.sides),
            [owner, rows[0], cols[0], rows[1], cols[1]],
            [Whole(tok), up, Whole(cot)],
            outs,
            [group_acc, pltpu.VMEM((group_blocks, BLK, row_count), jnp.bfloat16)],
            2 * flops,
            2 * block_bytes + side * (4 * model_blocks + 6 * group_blocks),
            [0, 0, devices],
        )

    def grad_pre_of(rows, cols, cot, down, slope, tok_turned):
        return run(
            functools.partial(grad_pre_kernel, down.sides),
            [owner, rows[1], cols[1], rows[0], cols[0]],
            [Whole(cot), down, Whole(slope), Whole(tok_turned)],
            [shape(group_cube, jnp.bfloat16), terms_shape],
            [group_acc],
            2 * flops,
            2 * block_bytes + side * (4 * model_blocks + 6 * group_blocks),
            [0, devices],
        )

    def width(contract, rows, cols, x, weights):
        outs = [shape((row_count, model_width), jnp.bfloat16)]
        nbytes = block_bytes + side * (2 * model_blocks + 2 * group_blocks)
        kernel = functools.partial(width_kernel, contract, weights.sides)
        return run(kernel, [rows, cols], [Whole(x), weights], outs, [model_acc], flops, nbytes)[0]

    is_live = codes >= 0
    row_codes = jnp.where(is_live, codes // group_blocks, 0)
    col_codes = jnp.where(is_live, codes % group_blocks, -1)

    if BLK % (PACK * devices) == 0 and slots <= BLK:
        here = me.reshape(1).astype(jnp.int32)
        piece = BLK // devices

        note = jnp.concatenate([row_codes, col_codes]).reshape(4, slots).astype(jnp.bfloat16)
        note = jnp.pad(note, ((0, piece - 4), (0, BLK - slots)))
        messages = split_blocks(here, up_slots, down_slots, note, devices)
        parts = [messages[0]] + [
            lax.ppermute(messages[s], "dp", [(i, i ^ s) for i in range(devices)]) for s in range(1, devices)
        ]
        notes = jnp.stack([part[2 * slots, :4, :slots] for part in parts], axis=1).astype(jnp.int32)
        pick, rows, cols = tables(notes[:2], notes[2:], index ^ me)
        place_of = (pick // slots) * (2 * slots) + pick % slots
        pick = place_of + jnp.array([[0], [slots]], jnp.int32)

        tokens, cotangent = tie((tokens, cotangent), parts[1])
        tok = lax.all_gather(tokens, "tensor", axis=0, tiled=True)
        cot = lax.all_gather(cotangent, "tensor", axis=0, tiled=True)

        def onward(pair):
            return lax.ppermute(pair[0], "dp", ahead), lax.ppermute(pair[1], "dp", behind)

        def ring(pair):
            pairs = [pair]
            for _ in range(1, devices):
                pairs.append(onward(pairs[-1]))
            return Joined(*zip(*pairs, strict=True), (from_ahead, from_behind))

        packed = pack_pieces(pick, parts, slots, live)
        up, down = ring(packed[:2]), ring(packed[2:])
    else:

        def everywhere(x, axis):
            return lax.all_gather(x, "dp", axis=axis, tiled=True)

        pick, rows, cols = tables(everywhere(row_codes, 1), everywhere(col_codes, 1), index)
        tok = lax.all_gather(tokens, "tensor", axis=0, tiled=True)
        cot = lax.all_gather(cotangent, "tensor", axis=0, tiled=True)
        up = Whole(jnp.take(everywhere(up_slots, 0), pick[0], axis=0))
        down = Whole(jnp.take(everywhere(down_slots, 0), pick[1], axis=0))

    hid, slope, terms = hidden_of(rows, cols, tok, cot, up)
    down_sum = RingSum(terms, ahead, behind)
    down_sum.step()
    grad_pre, terms = grad_pre_of(rows, cols, tie(cot, down_sum.run), down, slope, tok.T)
    up_sum = RingSum(terms, ahead, behind)
    up_sum.step()
    out_part = width(0, rows[1], cols[1], tie(hid, up_sum.run), down)
    up_sum.step()
    in_part = width(1, rows[0], cols[0], tie(grad_pre, out_part, up_sum.run), up)
    outputs = lax.psum_scatter(out_part, "tensor", scatter_dimension=0, tiled=True)
    input_grads = lax.psum_scatter(in_part, "tensor", scatter_dimension=0, tiled=True)
    while down_sum.steps_left():
        down_sum.step()
    while up_sum.steps_left():
        up_sum.step()

    scale = 1.0 / math.sqrt(devices * row_count)
    grads_shape = (1, 1, mean, BLK, BLK)
    up_grads = (up_sum.total() * scale).reshape(grads_shape)
    down_grads = (down_sum.total() * scale).reshape(grads_shape)
    return (outputs, input_grads, up_grads, down_grads)


def solution(mesh):
    return jax.shard_map(
        shards,
        mesh=mesh,
        in_specs=(
            P(("dp", "tensor"), None),
            P(("dp", "tensor"), None),
            P("dp", "tensor", None, None, None),
            P("dp", "tensor", None),
            P("dp", "tensor", None, None, None),
            P("dp", "tensor", None),
        ),
        out_specs=(
            P(("dp", "tensor"), None),
            P(("dp", "tensor"), None),
            P("dp", "tensor", None, None, None),
            P("dp", "tensor", None, None, None),
        ),
        check_vma=False,
    )
```

```python
import functools
import math

import jax
import jax.numpy as jnp
from jax import lax
from jax.experimental import pallas as pl
from jax.experimental.pallas import tpu as pltpu
from jax.sharding import PartitionSpec as P

FF = 16384
BLK = 128
PACK = 16
WEIGHT = 16
VMEM_LIMIT = 56 << 20

gelu_root = 0.7978845608028654
gelu_cubic = 0.044715

SMEM_SPEC = pl.BlockSpec(memory_space=pltpu.SMEM)
ANY_SPEC = pl.BlockSpec(memory_space=pl.ANY)


def ring_order(devices):
    evens = list(range(0, devices, 2))
    odds = list(range(1, devices, 2))
    return evens + odds[::-1]


def ring_pairs(devices):
    order = ring_order(devices)
    ahead = [(order[i], order[(i + 1) % devices]) for i in range(devices)]
    behind = [(b, a) for a, b in ahead]
    return ahead, behind


def shape(dims, dtype):
    return jax.ShapeDtypeStruct(tuple(dims), dtype)


def dot(a, b, ca, cb):
    return lax.dot_general(a, b, (((ca,), (cb,)), ((), ())), preferred_element_type=jnp.float32)


def unroll_of(count):
    return math.gcd(count, 8)


class Whole:
    sides = 1

    def __init__(self, array):
        self.arrays, self.tables = [array], []
        self.held = pltpu.VMEM(array.shape, array.dtype)

    def copies(self, tables, refs, held, sems):
        return [pltpu.make_async_copy(refs[0], held, sems.at[0])]


class Parts:
    def __init__(self, arrays, slots):
        self.arrays, self.tables, self.slots = list(arrays), [], slots
        first = arrays[0]
        self.held = pltpu.VMEM((len(arrays) * slots, *first.shape[1:]), first.dtype)

    def copies(self, tables, refs, held, sems):
        slots = self.slots
        return [
            pltpu.make_async_copy(ref.at[pl.ds(0, slots)], held.at[pl.ds(i * slots, slots)], sems.at[i])
            for i, ref in enumerate(refs)
        ]


class Joined:
    sides = 2

    def __init__(self, first, second, tables):
        self.arrays, self.tables = [*first, *second], list(tables)
        half = first[0].shape[0]
        self.held = pltpu.VMEM((2 * half, BLK, BLK), first[0].dtype)

    def copies(self, tables, refs, held, sems):
        half, piece, _ = refs[0].shape
        out = []
        for i, ref in enumerate(refs):
            side, j = divmod(i, len(refs) // 2)
            start = pl.multiple_of(tables[side][j] * piece, piece)
            to = held.at[pl.ds(side * half, half), pl.ds(start, piece), :]
            out.append(pltpu.make_async_copy(ref, to, sems.at[i]))
        return out


def run(kernel, small, items, outs, scratch=(), flops=0, nbytes=0, chunks=None):
    tables = [t for item in items for t in item.tables]
    arrays = [x for item in items for x in item.arrays]
    chunks = chunks or [0] * len(outs)

    def body(*refs):
        refs = list(refs)

        def take(n):
            taken = refs[:n]
            del refs[:n]
            return taken

        small_refs = take(len(small))
        table_refs = [take(len(item.tables)) for item in items]
        array_refs = [take(len(item.arrays)) for item in items]
        out_refs = take(len(outs))
        held_refs = take(len(items))
        result_refs = take(len(outs))
        scratch_refs = take(len(scratch))
        in_sems, out_sems = refs[: len(items)], refs[len(items) :]
        fetches = [
            item.copies(t, x, held, sems)
            for item, t, x, held, sems in zip(items, table_refs, array_refs, held_refs, in_sems, strict=True)
        ]
        for copies in fetches:
            for copy in copies:
                copy.start()

        def need(*which, part=(0, 1)):
            for i in which:
                size = len(fetches[i]) // part[1]
                for copy in fetches[i][part[0] * size : (part[0] + 1) * size]:
                    copy.wait()

        sent = {}

        def send(i, q=None):
            result, out, sem = result_refs[i], out_refs[i], out_sems[i].at[q or 0]
            if q is not None:
                result, out = result.at[q], out.at[q]
            sent[i, q] = pltpu.make_async_copy(result, out, sem)
            sent[i, q].start()

        kernel(need, send, *small_refs, *held_refs, *result_refs, *scratch_refs)
        for i, count in enumerate(chunks):
            for q in range(count) if count else [None]:
                if (i, q) not in sent:
                    send(i, q)
        for copy in sent.values():
            copy.wait()

    return pl.pallas_call(
        body,
        out_shape=list(outs),
        in_specs=[SMEM_SPEC] * (len(small) + len(tables)) + [ANY_SPEC] * len(arrays),
        out_specs=[ANY_SPEC] * len(outs),
        scratch_shapes=[
            *(item.held for item in items),
            *(pltpu.VMEM(x.shape, x.dtype) for x in outs),
            *scratch,
            *(pltpu.SemaphoreType.DMA((len(item.arrays),)) for item in items),
            *(pltpu.SemaphoreType.DMA((max(1, count),)) for count in chunks),
        ],
        compiler_params=pltpu.CompilerParams(vmem_limit_bytes=VMEM_LIMIT),
        cost_estimate=pl.CostEstimate(flops=flops, bytes_accessed=nbytes, transcendentals=0),
    )(*small, *tables, *arrays)


def split_blocks(me, up, down, note, devices):
    slots = up.shape[0]
    piece = BLK // devices

    def kernel(need, send, me_ref, up_ref, down_ref, note_ref, *outs):
        need(0, 1, 2)
        for step, out in enumerate(outs):
            start = pl.multiple_of((me_ref[0] ^ step) * piece, piece)
            out[:slots] = up_ref[:, pl.ds(start, piece), :]
            out[slots : 2 * slots] = down_ref[:, pl.ds(start, piece), :]
            out[2 * slots] = note_ref[...]
            send(step)

    out = [shape((2 * slots + 1, piece, BLK), up.dtype)] * devices
    return run(kernel, [me], [Whole(up), Whole(down), Whole(note)], out, nbytes=8 * up.size)


def pack_pieces(pick, parts, slots, live):
    piece = parts[0].shape[1]
    half = live // 2
    unroll = unroll_of(half)

    def kernel(need, send, up_pick, down_pick, held, *outs):
        need(0)
        for which, picked in enumerate((up_pick, down_pick)):
            ahead, behind = outs[2 * which : 2 * which + 2]

            def body(i, carry, picked=picked, ahead=ahead, behind=behind):
                for u in range(unroll):
                    k = i * unroll + u
                    ahead[k] = held[picked[k]]
                    behind[k] = held[picked[half + k]]
                return carry

            lax.fori_loop(0, half // unroll, body, 0)
            send(2 * which)
            send(2 * which + 1)

    out = [shape((half, piece, BLK), parts[0].dtype)] * 4
    items = [Parts(parts, 2 * slots)]
    return run(kernel, [pick[0], pick[1]], items, out, nbytes=6 * len(parts) * slots * piece * BLK)


def lanes(ref, block):
    return ref[:, pl.ds(pl.multiple_of(block * BLK, BLK), BLK)]


def sum_blocks(acc, live, sides, target, term, fetch):
    acc[...] = jnp.zeros_like(acc)
    count = live // sides
    for side in range(sides):
        fetch(side)
        for k in range(side * count, (side + 1) * count):
            acc[target(k)] += term(k)


def fetch_of(need, item, sides):
    return lambda side: need(item, part=(side, sides))


def down_terms(owner_ref, rows_ref, cols_ref, turned_ref, cot_ref, out_ref, send):
    devices, mean = out_ref.shape[:2]
    for q in range(devices):
        base = owner_ref[q] * mean
        for j in range(mean):
            row, col = rows_ref[base + j], cols_ref[base + j]
            out_ref[q, j] = dot(turned_ref[col], lanes(cot_ref, row), 1, 0).astype(jnp.bfloat16)
        send(q)


def up_terms(owner_ref, rows_ref, cols_ref, turned_ref, grad_ref, out_ref, send):
    devices, mean = out_ref.shape[:2]
    for q in range(devices):
        base = owner_ref[q] * mean
        for j in range(mean):
            row, col = rows_ref[base + j], cols_ref[base + j]
            turned = turned_ref[pl.ds(pl.multiple_of(row * BLK, BLK), BLK), :]
            out_ref[q, j] = dot(turned, grad_ref[col], 1, 0).astype(jnp.bfloat16)
        send(q)


def hidden_kernel(sides, need, send, owner, rows, cols, down_rows, down_cols, tok, w, cot, hid, slope, out, acc, turned):
    need(0)
    fetch = fetch_of(need, 1, sides)
    sum_blocks(acc, w.shape[0], sides, lambda k: cols[k], lambda k: dot(lanes(tok, rows[k]), w[k], 1, 0), fetch)

    def body(c, carry):
        values = acc[c]
        tanh = jnp.tanh(gelu_root * (values + gelu_cubic * values * values * values))
        hidden = 0.5 * values * (1.0 + tanh)
        hid[c] = hidden.astype(jnp.bfloat16)
        turned[c] = hidden.T.astype(jnp.bfloat16)
        slope[c] = 0.5 * (1.0 + tanh) + 0.5 * values * (1.0 - tanh * tanh) * gelu_root * (
            1.0 + 3.0 * gelu_cubic * values * values
        )
        return carry

    lax.fori_loop(0, acc.shape[0], body, 0)
    send(0)
    send(1)
    need(2)
    down_terms(owner, down_rows, down_cols, turned, cot, out, lambda q: send(2, q))


def grad_pre_kernel(sides, need, send, owner, rows, cols, up_rows, up_cols, cot, w, slope, tok_turned, grad, out, acc):
    need(0)
    fetch = fetch_of(need, 1, sides)
    sum_blocks(acc, w.shape[0], sides, lambda k: cols[k], lambda k: dot(lanes(cot, rows[k]), w[k], 1, 1), fetch)
    need(2)

    def body(c, carry):
        grad[c] = (acc[c] * slope[c]).astype(jnp.bfloat16)
        return carry

    lax.fori_loop(0, acc.shape[0], body, 0)
    send(0)
    need(3)
    up_terms(owner, up_rows, up_cols, tok_turned, grad, out, lambda q: send(1, q))


def width_kernel(contract, sides, need, send, rows, cols, x, w, out, acc):
    need(0)
    fetch = fetch_of(need, 1, sides)
    sum_blocks(acc, w.shape[0], sides, lambda k: rows[k], lambda k: dot(x[cols[k]], w[k], 1, contract), fetch)
    for r in range(acc.shape[0]):
        out[:, r * BLK : (r + 1) * BLK] = acc[r].astype(jnp.bfloat16)


def tie(value, *others):
    return lax.optimization_barrier((value, others))[0]


class RingSum:
    def __init__(self, parts, ahead, behind):
        self.parts, self.ahead, self.behind = parts, ahead, behind
        self.devices = parts.shape[0]
        self.done = 0
        self.run = (self.low(0), self.high((self.devices - 2) % self.devices))

    def low(self, q):
        return self.parts[q, :, : BLK // 2]

    def high(self, q):
        return self.parts[q, :, BLK // 2 :]

    def step(self, *after):
        self.done += 1
        last = self.done == self.devices - 1
        a, b = (x.astype(jnp.bfloat16) for x in self.run)
        if after:
            a, b = tie((a, b), *after)
        a = lax.ppermute(a, "dp", self.ahead)
        b = lax.ppermute(b, "dp", self.behind)
        a = a.astype(jnp.float32) + self.low(self.done).astype(jnp.float32)
        q = self.done if last else self.devices - 2 - self.done
        b = b.astype(jnp.float32) + self.high(q).astype(jnp.float32)
        if not last:
            a, b = a.astype(jnp.bfloat16), b.astype(jnp.bfloat16)
        self.run = (a, b)
        return self.run

    def steps_left(self):
        return self.devices - 1 - self.done

    def total(self):
        return jnp.concatenate(self.run, axis=1)


def tables(rows, cols, owners):
    _, devices, slots = rows.shape
    live = devices * (slots // 2)
    counts = jnp.sum((cols >= 0).astype(jnp.int32), axis=2)
    earlier = owners[None, :] < owners[:, None]
    offset = jnp.sum(jnp.where(earlier[None], counts[:, None, :], 0), axis=2)
    within = jnp.arange(live, dtype=jnp.int32)[None, :, None] - offset[:, None, :]
    held = (within >= 0) & (within < counts[:, None, :])
    base = jnp.arange(devices, dtype=jnp.int32) * slots
    pick = jnp.sum(jnp.where(held, within + base[None, None, :], 0), axis=2)
    every = jnp.arange(devices * slots, dtype=jnp.int32)
    chosen = every[None, None, :] == pick[:, :, None]
    at = [jnp.sum(jnp.where(chosen, x.reshape(2, 1, devices * slots), 0), axis=2) for x in (rows, cols)]
    return pick, at[0], at[1]


def shards(tokens, cotangent, up_blocks, up_place, down_blocks, down_place):
    devices = lax.axis_size("dp")
    me = lax.axis_index("dp")
    slots = up_place.shape[2]
    mean = slots // 2
    live = devices * mean
    group_blocks = FF // BLK // lax.axis_size("tensor")
    row_count = tokens.shape[0] * lax.axis_size("tensor")
    model_width = tokens.shape[1]
    model_blocks = model_width // BLK

    order = ring_order(devices)
    place = {d: i for i, d in enumerate(order)}
    ahead, behind = ring_pairs(devices)
    nav = jnp.array(
        [
            [
                [order[(place[d] - j) % devices] for j in range(devices)],
                [order[(place[d] + j) % devices] for j in range(devices)],
                [order[(place[d] - 1 - j) % devices] for j in range(devices)],
            ]
            for d in range(devices)
        ],
        jnp.int32,
    )[me]
    from_ahead, from_behind, owner = nav[0], nav[1], nav[2]
    index = jnp.arange(devices, dtype=jnp.int32)
    up_slots = up_blocks.reshape(slots, BLK, BLK)
    down_slots = down_blocks.reshape(slots, BLK, BLK)
    codes = jnp.stack([up_place.reshape(1, slots), down_place.reshape(1, slots)])

    flops = 2 * live * row_count * BLK * BLK * WEIGHT
    block_bytes = live * BLK * BLK * 2
    side = row_count * BLK
    group_acc = pltpu.VMEM((group_blocks, row_count, BLK), jnp.float32)
    model_acc = pltpu.VMEM((model_blocks, row_count, BLK), jnp.float32)

    group_cube = (group_blocks, row_count, BLK)
    terms_shape = shape((devices, mean, BLK, BLK), jnp.bfloat16)

    def hidden_of(rows, cols, tok, cot, up):
        outs = [shape(group_cube, jnp.bfloat16), shape(group_cube, jnp.float32), terms_shape]
        return run(
            functools.partial(hidden_kernel, up.sides),
            [owner, rows[0], cols[0], rows[1], cols[1]],
            [Whole(tok), up, Whole(cot)],
            outs,
            [group_acc, pltpu.VMEM((group_blocks, BLK, row_count), jnp.bfloat16)],
            2 * flops,
            2 * block_bytes + side * (4 * model_blocks + 6 * group_blocks),
            [0, 0, devices],
        )

    def grad_pre_of(rows, cols, cot, down, slope, tok_turned):
        return run(
            functools.partial(grad_pre_kernel, down.sides),
            [owner, rows[1], cols[1], rows[0], cols[0]],
            [Whole(cot), down, Whole(slope), Whole(tok_turned)],
            [shape(group_cube, jnp.bfloat16), terms_shape],
            [group_acc],
            2 * flops,
            2 * block_bytes + side * (4 * model_blocks + 6 * group_blocks),
            [0, devices],
        )

    def width(contract, rows, cols, x, weights):
        outs = [shape((row_count, model_width), jnp.bfloat16)]
        nbytes = block_bytes + side * (2 * model_blocks + 2 * group_blocks)
        kernel = functools.partial(width_kernel, contract, weights.sides)
        return run(kernel, [rows, cols], [Whole(x), weights], outs, [model_acc], flops, nbytes)[0]

    is_live = codes >= 0
    row_codes = jnp.where(is_live, codes // group_blocks, 0)
    col_codes = jnp.where(is_live, codes % group_blocks, -1)

    if BLK % (PACK * devices) == 0 and slots <= BLK:
        here = me.reshape(1).astype(jnp.int32)
        piece = BLK // devices

        note = jnp.concatenate([row_codes, col_codes]).reshape(4, slots).astype(jnp.bfloat16)
        note = jnp.pad(note, ((0, piece - 4), (0, BLK - slots)))
        messages = split_blocks(here, up_slots, down_slots, note, devices)
        parts = [messages[0]] + [
            lax.ppermute(messages[s], "dp", [(i, i ^ s) for i in range(devices)]) for s in range(1, devices)
        ]
        notes = jnp.stack([part[2 * slots, :4, :slots] for part in parts], axis=1).astype(jnp.int32)
        pick, rows, cols = tables(notes[:2], notes[2:], index ^ me)
        place_of = (pick // slots) * (2 * slots) + pick % slots
        pick = place_of + jnp.array([[0], [slots]], jnp.int32)

        tokens, cotangent = tie((tokens, cotangent), parts[1])
        tok = lax.all_gather(tokens, "tensor", axis=0, tiled=True)
        cot = lax.all_gather(cotangent, "tensor", axis=0, tiled=True)

        def onward(pair):
            return lax.ppermute(pair[0], "dp", ahead), lax.ppermute(pair[1], "dp", behind)

        packed = pack_pieces(pick, parts, slots, live)
        tok_turned = tok.T

        up_ring, down_ring = [tuple(packed[:2])], [tuple(packed[2:])]
        for s in range(1, devices):
            up_ring.append(onward(tie(up_ring[-1], tok_turned) if s == devices // 2 else up_ring[-1]))
            down_ring.append(onward(down_ring[-1]))
        up, down = (Joined(*zip(*pairs, strict=True), (from_ahead, from_behind)) for pairs in (up_ring, down_ring))
    else:

        def everywhere(x, axis):
            return lax.all_gather(x, "dp", axis=axis, tiled=True)

        pick, rows, cols = tables(everywhere(row_codes, 1), everywhere(col_codes, 1), index)
        tok = lax.all_gather(tokens, "tensor", axis=0, tiled=True)
        cot = lax.all_gather(cotangent, "tensor", axis=0, tiled=True)
        tok_turned = tok.T
        up = Whole(jnp.take(everywhere(up_slots, 0), pick[0], axis=0))
        down = Whole(jnp.take(everywhere(down_slots, 0), pick[1], axis=0))

    hid, slope, terms = hidden_of(rows, cols, tok, cot, up)
    down_sum = RingSum(terms, ahead, behind)
    down_sum.step()
    grad_pre, terms = grad_pre_of(rows, cols, cot, down, slope, tok_turned)
    up_sum = RingSum(terms, ahead, behind)
    up_sum.step()
    out_part = width(0, rows[1], cols[1], tie(hid, up_sum.run), down)
    up_sum.step()
    in_part = width(1, rows[0], cols[0], tie(grad_pre, out_part, up_sum.run), up)
    outputs = lax.psum_scatter(out_part, "tensor", scatter_dimension=0, tiled=True)
    input_grads = lax.psum_scatter(in_part, "tensor", scatter_dimension=0, tiled=True)
    while down_sum.steps_left():
        down_sum.step()
    while up_sum.steps_left():
        up_sum.step()

    scale = 1.0 / math.sqrt(devices * row_count)
    grads_shape = (1, 1, mean, BLK, BLK)
    up_grads = (up_sum.total() * scale).reshape(grads_shape)
    down_grads = (down_sum.total() * scale).reshape(grads_shape)
    return (outputs, input_grads, up_grads, down_grads)


def solution(mesh):
    return jax.shard_map(
        shards,
        mesh=mesh,
        in_specs=(
            P(("dp", "tensor"), None),
            P(("dp", "tensor"), None),
            P("dp", "tensor", None, None, None),
            P("dp", "tensor", None),
            P("dp", "tensor", None, None, None),
            P("dp", "tensor", None),
        ),
        out_specs=(
            P(("dp", "tensor"), None),
            P(("dp", "tensor"), None),
            P("dp", "tensor", None, None, None),
            P("dp", "tensor", None, None, None),
        ),
        check_vma=False,
    )
```

```python
import functools
import math

import jax
import jax.numpy as jnp
from jax import lax
from jax.experimental import pallas as pl
from jax.experimental.pallas import tpu as pltpu
from jax.sharding import PartitionSpec as P

FF = 16384
BLK = 128
PACK = 16
WEIGHT = 16
VMEM_LIMIT = 56 << 20

gelu_root = 0.7978845608028654
gelu_cubic = 0.044715

SMEM_SPEC = pl.BlockSpec(memory_space=pltpu.SMEM)
ANY_SPEC = pl.BlockSpec(memory_space=pl.ANY)


def ring_order(devices):
    evens = list(range(0, devices, 2))
    odds = list(range(1, devices, 2))
    return evens + odds[::-1]


def ring_pairs(devices):
    order = ring_order(devices)
    ahead = [(order[i], order[(i + 1) % devices]) for i in range(devices)]
    behind = [(b, a) for a, b in ahead]
    return ahead, behind


def shape(dims, dtype):
    return jax.ShapeDtypeStruct(tuple(dims), dtype)


def dot(a, b, ca, cb):
    return lax.dot_general(a, b, (((ca,), (cb,)), ((), ())), preferred_element_type=jnp.float32)


def unroll_of(count):
    return math.gcd(count, 8)


class Whole:
    sides = 1

    def __init__(self, array):
        self.arrays, self.tables = [array], []
        self.held = pltpu.VMEM(array.shape, array.dtype)

    def copies(self, tables, refs, held, sems):
        return [pltpu.make_async_copy(refs[0], held, sems.at[0])]


class Parts:
    def __init__(self, arrays, slots):
        self.arrays, self.tables, self.slots = list(arrays), [], slots
        first = arrays[0]
        self.held = pltpu.VMEM((len(arrays) * slots, *first.shape[1:]), first.dtype)

    def copies(self, tables, refs, held, sems):
        slots = self.slots
        return [
            pltpu.make_async_copy(ref.at[pl.ds(0, slots)], held.at[pl.ds(i * slots, slots)], sems.at[i])
            for i, ref in enumerate(refs)
        ]


class Joined:
    sides = 2

    def __init__(self, first, second, tables):
        self.arrays, self.tables = [*first, *second], list(tables)
        half = first[0].shape[0]
        self.held = pltpu.VMEM((2 * half, BLK, BLK), first[0].dtype)

    def copies(self, tables, refs, held, sems):
        half, piece, _ = refs[0].shape
        out = []
        for i, ref in enumerate(refs):
            side, j = divmod(i, len(refs) // 2)
            start = pl.multiple_of(tables[side][j] * piece, piece)
            to = held.at[pl.ds(side * half, half), pl.ds(start, piece), :]
            out.append(pltpu.make_async_copy(ref, to, sems.at[i]))
        return out


def run(kernel, small, items, outs, scratch=(), flops=0, nbytes=0, chunks=None):
    tables = [t for item in items for t in item.tables]
    arrays = [x for item in items for x in item.arrays]
    chunks = chunks or [0] * len(outs)

    def body(*refs):
        refs = list(refs)

        def take(n):
            taken = refs[:n]
            del refs[:n]
            return taken

        small_refs = take(len(small))
        table_refs = [take(len(item.tables)) for item in items]
        array_refs = [take(len(item.arrays)) for item in items]
        out_refs = take(len(outs))
        held_refs = take(len(items))
        result_refs = take(len(outs))
        scratch_refs = take(len(scratch))
        in_sems, out_sems = refs[: len(items)], refs[len(items) :]
        fetches = [
            item.copies(t, x, held, sems)
            for item, t, x, held, sems in zip(items, table_refs, array_refs, held_refs, in_sems, strict=True)
        ]
        for copies in fetches:
            for copy in copies:
                copy.start()

        def need(*which, part=(0, 1)):
            for i in which:
                size = len(fetches[i]) // part[1]
                for copy in fetches[i][part[0] * size : (part[0] + 1) * size]:
                    copy.wait()

        sent = {}

        def send(i, q=None):
            result, out, sem = result_refs[i], out_refs[i], out_sems[i].at[q or 0]
            if q is not None:
                result, out = result.at[q], out.at[q]
            sent[i, q] = pltpu.make_async_copy(result, out, sem)
            sent[i, q].start()

        kernel(need, send, *small_refs, *held_refs, *result_refs, *scratch_refs)
        for i, count in enumerate(chunks):
            for q in range(count) if count else [None]:
                if (i, q) not in sent:
                    send(i, q)
        for copy in sent.values():
            copy.wait()

    return pl.pallas_call(
        body,
        out_shape=list(outs),
        in_specs=[SMEM_SPEC] * (len(small) + len(tables)) + [ANY_SPEC] * len(arrays),
        out_specs=[ANY_SPEC] * len(outs),
        scratch_shapes=[
            *(item.held for item in items),
            *(pltpu.VMEM(x.shape, x.dtype) for x in outs),
            *scratch,
            *(pltpu.SemaphoreType.DMA((len(item.arrays),)) for item in items),
            *(pltpu.SemaphoreType.DMA((max(1, count),)) for count in chunks),
        ],
        compiler_params=pltpu.CompilerParams(vmem_limit_bytes=VMEM_LIMIT),
        cost_estimate=pl.CostEstimate(flops=flops, bytes_accessed=nbytes, transcendentals=0),
    )(*small, *tables, *arrays)


def split_blocks(me, up, down, note, devices):
    slots = up.shape[0]
    piece = BLK // devices

    def kernel(need, send, me_ref, up_ref, down_ref, note_ref, *outs):
        need(0, 1, 2)
        for step, out in enumerate(outs):
            start = pl.multiple_of((me_ref[0] ^ step) * piece, piece)
            out[:slots] = up_ref[:, pl.ds(start, piece), :]
            out[slots : 2 * slots] = down_ref[:, pl.ds(start, piece), :]
            out[2 * slots] = note_ref[...]
            send(step)

    out = [shape((2 * slots + 1, piece, BLK), up.dtype)] * devices
    return run(kernel, [me], [Whole(up), Whole(down), Whole(note)], out, nbytes=8 * up.size)


def pack_pieces(pick, parts, slots, live):
    piece = parts[0].shape[1]
    half = live // 2
    unroll = unroll_of(half)

    def kernel(need, send, up_pick, down_pick, held, *outs):
        need(0)
        for which, picked in enumerate((up_pick, down_pick)):
            ahead, behind = outs[2 * which : 2 * which + 2]

            def body(i, carry, picked=picked, ahead=ahead, behind=behind):
                for u in range(unroll):
                    k = i * unroll + u
                    ahead[k] = held[picked[k]]
                    behind[k] = held[picked[half + k]]
                return carry

            lax.fori_loop(0, half // unroll, body, 0)
            send(2 * which)
            send(2 * which + 1)

    out = [shape((half, piece, BLK), parts[0].dtype)] * 4
    items = [Parts(parts, 2 * slots)]
    return run(kernel, [pick[0], pick[1]], items, out, nbytes=6 * len(parts) * slots * piece * BLK)


def lanes(ref, block):
    return ref[:, pl.ds(pl.multiple_of(block * BLK, BLK), BLK)]


def sum_blocks(acc, live, sides, target, term, fetch):
    acc[...] = jnp.zeros_like(acc)
    count = live // sides
    for side in range(sides):
        fetch(side)
        for k in range(side * count, (side + 1) * count):
            acc[target(k)] += term(k)


def fetch_of(need, item, sides):
    return lambda side: need(item, part=(side, sides))


def down_terms(owner_ref, rows_ref, cols_ref, turned_ref, cot_ref, out_ref, send):
    devices, mean = out_ref.shape[:2]
    for q in range(devices):
        base = owner_ref[q] * mean
        for j in range(mean):
            row, col = rows_ref[base + j], cols_ref[base + j]
            out_ref[q, j] = dot(turned_ref[col], lanes(cot_ref, row), 1, 0).astype(jnp.bfloat16)
        send(q)


def up_terms(owner_ref, rows_ref, cols_ref, turned_ref, grad_ref, out_ref, send):
    devices, mean = out_ref.shape[:2]
    for q in range(devices):
        base = owner_ref[q] * mean
        for j in range(mean):
            row, col = rows_ref[base + j], cols_ref[base + j]
            turned = turned_ref[pl.ds(pl.multiple_of(row * BLK, BLK), BLK), :]
            out_ref[q, j] = dot(turned, grad_ref[col], 1, 0).astype(jnp.bfloat16)
        send(q)


def hidden_kernel(sides, need, send, owner, rows, cols, down_rows, down_cols, tok, w, cot, hid, slope, out, acc, turned):
    need(0)
    fetch = fetch_of(need, 1, sides)
    sum_blocks(acc, w.shape[0], sides, lambda k: cols[k], lambda k: dot(lanes(tok, rows[k]), w[k], 1, 0), fetch)

    def body(c, carry):
        values = acc[c]
        tanh = jnp.tanh(gelu_root * (values + gelu_cubic * values * values * values))
        hidden = 0.5 * values * (1.0 + tanh)
        hid[c] = hidden.astype(jnp.bfloat16)
        turned[c] = hidden.T.astype(jnp.bfloat16)
        slope[c] = 0.5 * (1.0 + tanh) + 0.5 * values * (1.0 - tanh * tanh) * gelu_root * (
            1.0 + 3.0 * gelu_cubic * values * values
        )
        return carry

    lax.fori_loop(0, acc.shape[0], body, 0)
    send(0)
    send(1)
    need(2)
    down_terms(owner, down_rows, down_cols, turned, cot, out, lambda q: send(2, q))


def grad_pre_kernel(sides, need, send, owner, rows, cols, up_rows, up_cols, cot, w, slope, tok_turned, grad, out, acc):
    need(0)
    fetch = fetch_of(need, 1, sides)
    sum_blocks(acc, w.shape[0], sides, lambda k: cols[k], lambda k: dot(lanes(cot, rows[k]), w[k], 1, 1), fetch)
    need(2)

    def body(c, carry):
        grad[c] = (acc[c] * slope[c]).astype(jnp.bfloat16)
        return carry

    lax.fori_loop(0, acc.shape[0], body, 0)
    send(0)
    need(3)
    up_terms(owner, up_rows, up_cols, tok_turned, grad, out, lambda q: send(1, q))


def width_kernel(contract, sides, need, send, rows, cols, x, w, out, acc):
    need(0)
    fetch = fetch_of(need, 1, sides)
    sum_blocks(acc, w.shape[0], sides, lambda k: rows[k], lambda k: dot(x[cols[k]], w[k], 1, contract), fetch)
    for r in range(acc.shape[0]):
        out[:, r * BLK : (r + 1) * BLK] = acc[r].astype(jnp.bfloat16)


def tie(value, *others):
    return lax.optimization_barrier((value, others))[0]


def tensor_masks():
    masks = []
    mask = 1
    while mask < lax.axis_size("tensor"):
        masks.append(mask)
        mask *= 2
    return masks


def swap(value, mask):
    devices = lax.axis_size("tensor")
    return lax.ppermute(value, "tensor", [(i, i ^ mask) for i in range(devices)])


def gather_rows(value):
    for mask in reversed(tensor_masks()):
        value = jnp.concatenate([value, swap(value, mask)], axis=1)
    return value


def spread_sum(value):
    for mask in tensor_masks():
        half = value.shape[1] // 2
        other = swap(value[:, half:], mask)
        value = (value[:, :half].astype(jnp.float32) + other.astype(jnp.float32)).astype(jnp.bfloat16)
    return value


class RingSum:
    def __init__(self, parts, ahead, behind):
        self.parts, self.ahead, self.behind = parts, ahead, behind
        self.devices = parts.shape[0]
        self.done = 0
        self.run = (self.low(0), self.high((self.devices - 2) % self.devices))

    def low(self, q):
        return self.parts[q, :, : BLK // 2]

    def high(self, q):
        return self.parts[q, :, BLK // 2 :]

    def step(self):
        self.send()
        self.add()

    def send(self):
        a, b = (x.astype(jnp.bfloat16) for x in self.run)
        self.run = lax.ppermute(a, "dp", self.ahead), lax.ppermute(b, "dp", self.behind)

    def add(self, *after):
        self.done += 1
        last = self.done == self.devices - 1
        a, b = tie(self.run, *after) if after else self.run
        a = a.astype(jnp.float32) + self.low(self.done).astype(jnp.float32)
        q = self.done if last else self.devices - 2 - self.done
        b = b.astype(jnp.float32) + self.high(q).astype(jnp.float32)
        if not last:
            a, b = a.astype(jnp.bfloat16), b.astype(jnp.bfloat16)
        self.run = (a, b)

    def steps_left(self):
        return self.devices - 1 - self.done

    def total(self):
        return jnp.concatenate(self.run, axis=1)


def tables(rows, cols, owners):
    _, devices, slots = rows.shape
    live = devices * (slots // 2)
    counts = jnp.sum((cols >= 0).astype(jnp.int32), axis=2)
    earlier = owners[None, :] < owners[:, None]
    offset = jnp.sum(jnp.where(earlier[None], counts[:, None, :], 0), axis=2)
    within = jnp.arange(live, dtype=jnp.int32)[None, :, None] - offset[:, None, :]
    held = (within >= 0) & (within < counts[:, None, :])
    base = jnp.arange(devices, dtype=jnp.int32) * slots
    pick = jnp.sum(jnp.where(held, within + base[None, None, :], 0), axis=2)
    every = jnp.arange(devices * slots, dtype=jnp.int32)
    chosen = every[None, None, :] == pick[:, :, None]
    at = [jnp.sum(jnp.where(chosen, x.reshape(2, 1, devices * slots), 0), axis=2) for x in (rows, cols)]
    return pick, at[0], at[1]


def shards(tokens, cotangent, up_blocks, up_place, down_blocks, down_place):
    devices = lax.axis_size("dp")
    me = lax.axis_index("dp")
    slots = up_place.shape[2]
    mean = slots // 2
    live = devices * mean
    group_blocks = FF // BLK // lax.axis_size("tensor")
    row_count = tokens.shape[0] * lax.axis_size("tensor")
    model_width = tokens.shape[1]
    model_blocks = model_width // BLK

    order = ring_order(devices)
    place = {d: i for i, d in enumerate(order)}
    ahead, behind = ring_pairs(devices)
    nav = jnp.array(
        [
            [
                [order[(place[d] - j) % devices] for j in range(devices)],
                [order[(place[d] + j) % devices] for j in range(devices)],
                [order[(place[d] - 1 - j) % devices] for j in range(devices)],
            ]
            for d in range(devices)
        ],
        jnp.int32,
    )[me]
    from_ahead, from_behind, owner = nav[0], nav[1], nav[2]
    index = jnp.arange(devices, dtype=jnp.int32)
    up_slots = up_blocks.reshape(slots, BLK, BLK)
    down_slots = down_blocks.reshape(slots, BLK, BLK)
    codes = jnp.stack([up_place.reshape(1, slots), down_place.reshape(1, slots)])

    flops = 2 * live * row_count * BLK * BLK * WEIGHT
    block_bytes = live * BLK * BLK * 2
    side = row_count * BLK
    group_acc = pltpu.VMEM((group_blocks, row_count, BLK), jnp.float32)
    model_acc = pltpu.VMEM((model_blocks, row_count, BLK), jnp.float32)

    group_cube = (group_blocks, row_count, BLK)
    terms_shape = shape((devices, mean, BLK, BLK), jnp.bfloat16)

    def hidden_of(rows, cols, tok, cot, up):
        outs = [shape(group_cube, jnp.bfloat16), shape(group_cube, jnp.float32), terms_shape]
        return run(
            functools.partial(hidden_kernel, up.sides),
            [owner, rows[0], cols[0], rows[1], cols[1]],
            [Whole(tok), up, Whole(cot)],
            outs,
            [group_acc, pltpu.VMEM((group_blocks, BLK, row_count), jnp.bfloat16)],
            2 * flops,
            2 * block_bytes + side * (4 * model_blocks + 6 * group_blocks),
            [0, 0, devices],
        )

    def grad_pre_of(rows, cols, cot, down, slope, tok_turned):
        return run(
            functools.partial(grad_pre_kernel, down.sides),
            [owner, rows[1], cols[1], rows[0], cols[0]],
            [Whole(cot), down, Whole(slope), Whole(tok_turned)],
            [shape(group_cube, jnp.bfloat16), terms_shape],
            [group_acc],
            2 * flops,
            2 * block_bytes + side * (4 * model_blocks + 6 * group_blocks),
            [0, devices],
        )

    def width(contract, rows, cols, x, weights):
        outs = [shape((row_count, model_width), jnp.bfloat16)]
        nbytes = block_bytes + side * (2 * model_blocks + 2 * group_blocks)
        kernel = functools.partial(width_kernel, contract, weights.sides)
        return run(kernel, [rows, cols], [Whole(x), weights], outs, [model_acc], flops, nbytes)[0]

    is_live = codes >= 0
    row_codes = jnp.where(is_live, codes // group_blocks, 0)
    col_codes = jnp.where(is_live, codes % group_blocks, -1)

    if BLK % (PACK * devices) == 0 and slots <= BLK:
        here = me.reshape(1).astype(jnp.int32)
        piece = BLK // devices

        note = jnp.concatenate([row_codes, col_codes]).reshape(4, slots).astype(jnp.bfloat16)
        note = jnp.pad(note, ((0, piece - 4), (0, BLK - slots)))
        messages = split_blocks(here, up_slots, down_slots, note, devices)
        parts = [messages[0]] * devices
        for step in range(1, devices):
            parts[step] = lax.ppermute(messages[step], "dp", [(i, i ^ step) for i in range(devices)])
        notes = jnp.stack([part[2 * slots, :4, :slots] for part in parts], axis=1).astype(jnp.int32)
        pick, rows, cols = tables(notes[:2], notes[2:], index ^ me)
        place_of = (pick // slots) * (2 * slots) + pick % slots
        pick = place_of + jnp.array([[0], [slots]], jnp.int32)

        tok, cot = gather_rows(tie(jnp.stack([tokens, cotangent]), parts[1]))

        def onward(pair):
            return lax.ppermute(pair[0], "dp", ahead), lax.ppermute(pair[1], "dp", behind)

        packed = pack_pieces(pick, parts, slots, live)
        tok_turned = tok.T

        up_ring, down_ring = [tuple(packed[:2])], [tuple(packed[2:])]
        for s in range(1, devices):
            up_ring.append(onward(tie(up_ring[-1], tok_turned) if s == devices // 2 else up_ring[-1]))
            down_ring.append(onward(down_ring[-1]))
        up, down = (Joined(*zip(*pairs, strict=True), (from_ahead, from_behind)) for pairs in (up_ring, down_ring))
    else:

        def everywhere(x, axis):
            return lax.all_gather(x, "dp", axis=axis, tiled=True)

        pick, rows, cols = tables(everywhere(row_codes, 1), everywhere(col_codes, 1), index)
        tok, cot = gather_rows(jnp.stack([tokens, cotangent]))
        tok_turned = tok.T
        up = Whole(jnp.take(everywhere(up_slots, 0), pick[0], axis=0))
        down = Whole(jnp.take(everywhere(down_slots, 0), pick[1], axis=0))

    hid, slope, terms = hidden_of(rows, cols, tok, cot, up)
    down_sum = RingSum(terms, ahead, behind)
    down_sum.send()
    grad_pre, terms = grad_pre_of(rows, cols, cot, down, slope, tok_turned)
    down_sum.add(grad_pre)
    up_sum = RingSum(terms, ahead, behind)
    up_sum.step()
    out_part = width(0, rows[1], cols[1], tie(hid, up_sum.run), down)
    up_sum.step()
    in_part = width(1, rows[0], cols[0], tie(grad_pre, out_part, up_sum.run), up)
    outputs, input_grads = spread_sum(jnp.stack([out_part, in_part]))
    while down_sum.steps_left():
        down_sum.step()
    while up_sum.steps_left():
        up_sum.step()

    scale = 1.0 / math.sqrt(devices * row_count)
    grads_shape = (1, 1, mean, BLK, BLK)
    up_grads = (up_sum.total() * scale).reshape(grads_shape)
    down_grads = (down_sum.total() * scale).reshape(grads_shape)
    return (outputs, input_grads, up_grads, down_grads)


def solution(mesh):
    return jax.shard_map(
        shards,
        mesh=mesh,
        in_specs=(
            P(("dp", "tensor"), None),
            P(("dp", "tensor"), None),
            P("dp", "tensor", None, None, None),
            P("dp", "tensor", None),
            P("dp", "tensor", None, None, None),
            P("dp", "tensor", None),
        ),
        out_specs=(
            P(("dp", "tensor"), None),
            P(("dp", "tensor"), None),
            P("dp", "tensor", None, None, None),
            P("dp", "tensor", None, None, None),
        ),
        check_vma=False,
    )
```

```python
import functools
import math

import jax
import jax.numpy as jnp
from jax import lax
from jax.experimental import pallas as pl
from jax.experimental.pallas import tpu as pltpu
from jax.sharding import PartitionSpec as P

FF = 16384
BLK = 128
PACK = 16
WEIGHT = 16
VMEM_LIMIT = 56 << 20

gelu_root = 0.7978845608028654
gelu_cubic = 0.044715

SMEM_SPEC = pl.BlockSpec(memory_space=pltpu.SMEM)
ANY_SPEC = pl.BlockSpec(memory_space=pl.ANY)


def ring_order(devices):
    evens = list(range(0, devices, 2))
    odds = list(range(1, devices, 2))
    return evens + odds[::-1]


def ring_pairs(devices):
    order = ring_order(devices)
    ahead = [(order[i], order[(i + 1) % devices]) for i in range(devices)]
    behind = [(b, a) for a, b in ahead]
    return ahead, behind


def shape(dims, dtype):
    return jax.ShapeDtypeStruct(tuple(dims), dtype)


def dot(a, b, ca, cb):
    return lax.dot_general(a, b, (((ca,), (cb,)), ((), ())), preferred_element_type=jnp.float32)


class Whole:
    sides = 1

    def __init__(self, array):
        self.arrays, self.tables = [array], []
        self.held = pltpu.VMEM(array.shape, array.dtype)

    def copies(self, tables, refs, held, sems):
        return [pltpu.make_async_copy(refs[0], held, sems.at[0])]


class Parts:
    def __init__(self, arrays, first, slots):
        self.arrays, self.tables, self.first, self.slots = list(arrays), [], first, slots
        self.held = pltpu.VMEM((len(arrays) * slots, *arrays[0].shape[1:]), arrays[0].dtype)

    def copies(self, tables, refs, held, sems):
        slots = self.slots
        return [
            pltpu.make_async_copy(ref.at[pl.ds(self.first, slots)], held.at[pl.ds(i * slots, slots)], sems.at[i])
            for i, ref in enumerate(refs)
        ]


class Joined:
    sides = 2

    def __init__(self, first, second, tables):
        self.arrays, self.tables = [*first, *second], list(tables)
        half = first[0].shape[0]
        self.held = pltpu.VMEM((2 * half, BLK, BLK), first[0].dtype)

    def copies(self, tables, refs, held, sems):
        half, piece, _ = refs[0].shape
        out = []
        for i, ref in enumerate(refs):
            side, j = divmod(i, len(refs) // 2)
            start = pl.multiple_of(tables[side][j] * piece, piece)
            to = held.at[pl.ds(side * half, half), pl.ds(start, piece), :]
            out.append(pltpu.make_async_copy(ref, to, sems.at[i]))
        return out


def run(kernel, small, items, outs, scratch=(), flops=0, nbytes=0, chunks=None):
    tables = [t for item in items for t in item.tables]
    arrays = [x for item in items for x in item.arrays]
    chunks = chunks or [0] * len(outs)

    def body(*refs):
        refs = list(refs)

        def take(n):
            taken = refs[:n]
            del refs[:n]
            return taken

        small_refs = take(len(small))
        table_refs = [take(len(item.tables)) for item in items]
        array_refs = [take(len(item.arrays)) for item in items]
        out_refs = take(len(outs))
        held_refs = take(len(items))
        result_refs = take(len(outs))
        scratch_refs = take(len(scratch))
        in_sems, out_sems = refs[: len(items)], refs[len(items) :]
        fetches = [
            item.copies(t, x, held, sems)
            for item, t, x, held, sems in zip(items, table_refs, array_refs, held_refs, in_sems, strict=True)
        ]
        for copies in fetches:
            for copy in copies:
                copy.start()

        def need(*which, part=(0, 1)):
            for i in which:
                size = len(fetches[i]) // part[1]
                for copy in fetches[i][part[0] * size : (part[0] + 1) * size]:
                    copy.wait()

        sent = {}

        def send(i, q=None):
            result, out, sem = result_refs[i], out_refs[i], out_sems[i].at[q or 0]
            if q is not None:
                result, out = result.at[q], out.at[q]
            sent[i, q] = pltpu.make_async_copy(result, out, sem)
            sent[i, q].start()

        kernel(need, send, *small_refs, *held_refs, *result_refs, *scratch_refs)
        for i, count in enumerate(chunks):
            for q in range(count) if count else [None]:
                if (i, q) not in sent:
                    send(i, q)
        for copy in sent.values():
            copy.wait()

    return pl.pallas_call(
        body,
        out_shape=list(outs),
        in_specs=[SMEM_SPEC] * (len(small) + len(tables)) + [ANY_SPEC] * len(arrays),
        out_specs=[ANY_SPEC] * len(outs),
        scratch_shapes=[
            *(item.held for item in items),
            *(pltpu.VMEM(x.shape, x.dtype) for x in outs),
            *scratch,
            *(pltpu.SemaphoreType.DMA((len(item.arrays),)) for item in items),
            *(pltpu.SemaphoreType.DMA((max(1, count),)) for count in chunks),
        ],
        compiler_params=pltpu.CompilerParams(vmem_limit_bytes=VMEM_LIMIT),
        cost_estimate=pl.CostEstimate(flops=flops, bytes_accessed=nbytes, transcendentals=0),
    )(*small, *tables, *arrays)


def split_blocks(me, up, down, codes, group_blocks, devices):
    slots = up.shape[0]
    piece = BLK // devices

    def kernel(need, send, me_ref, codes_ref, up_ref, down_ref, *refs):
        *outs, note = refs
        need(0)
        code = codes_ref[...]
        live = code >= 0
        known = jnp.where(live, code, 0)
        note[...] = jnp.zeros_like(note)
        note[0:2, 0:slots] = lax.div(known, jnp.full_like(known, group_blocks)).astype(jnp.float32)
        note[2:4, 0:slots] = jnp.where(live, lax.rem(known, jnp.full_like(known, group_blocks)), -1).astype(jnp.float32)
        need(1, 2)
        for step, out in enumerate(outs):
            start = pl.multiple_of((me_ref[0] ^ step) * piece, piece)
            out[:slots] = up_ref[:, pl.ds(start, piece), :]
            out[slots : 2 * slots] = down_ref[:, pl.ds(start, piece), :]
            out[2 * slots] = note[...].astype(jnp.bfloat16)
            send(step)

    out = [shape((2 * slots + 1, piece, BLK), up.dtype)] * devices
    items = [Whole(codes), Whole(up), Whole(down)]
    return run(kernel, [me], items, out, [pltpu.VMEM((piece, BLK), jnp.float32)], nbytes=8 * up.size)


def pack_pieces(pick, parts, first, slots, live):
    piece = parts[0].shape[1]
    half = live // 2

    def kernel(need, send, pick_ref, held, *outs):
        need(0)
        for side, out in enumerate(outs):
            for k in range(half):
                out[k] = held[pick_ref[side * half + k]]
            send(side)

    out = [shape((half, piece, BLK), parts[0].dtype)] * 2
    nbytes = 3 * len(parts) * slots * piece * BLK
    return tuple(run(kernel, [pick], [Parts(parts, first, slots)], out, nbytes=nbytes))


def lanes(ref, block):
    return ref[:, pl.ds(pl.multiple_of(block * BLK, BLK), BLK)]


def sum_blocks(acc, live, sides, target, term, fetch):
    acc[...] = jnp.zeros_like(acc)
    count = live // sides
    for side in range(sides):
        fetch(side)
        for k in range(side * count, (side + 1) * count):
            acc[target(k)] += term(k)


def fetch_of(need, item, sides):
    return lambda side: need(item, part=(side, sides))


def down_terms(owner_ref, rows_ref, cols_ref, turned_ref, cot_ref, out_ref, send):
    devices, mean = out_ref.shape[:2]
    for q in range(devices):
        base = owner_ref[q] * mean
        for j in range(mean):
            row, col = rows_ref[base + j], cols_ref[base + j]
            out_ref[q, j] = dot(turned_ref[col], lanes(cot_ref, row), 1, 0).astype(jnp.bfloat16)
        send(q)


def up_terms(owner_ref, rows_ref, cols_ref, turned_ref, grad_ref, out_ref, send):
    devices, mean = out_ref.shape[:2]
    for q in range(devices):
        base = owner_ref[q] * mean
        for j in range(mean):
            row, col = rows_ref[base + j], cols_ref[base + j]
            turned = turned_ref[pl.ds(pl.multiple_of(row * BLK, BLK), BLK), :]
            out_ref[q, j] = dot(turned, grad_ref[col], 1, 0).astype(jnp.bfloat16)
        send(q)


def hidden_kernel(sides, need, send, owner, rows, cols, down_rows, down_cols, tok, w, cot, hid, slope, out, acc, turned):
    need(0)
    fetch = fetch_of(need, 1, sides)
    sum_blocks(acc, w.shape[0], sides, lambda k: cols[k], lambda k: dot(lanes(tok, rows[k]), w[k], 1, 0), fetch)

    def body(c, carry):
        values = acc[c]
        tanh = jnp.tanh(gelu_root * (values + gelu_cubic * values * values * values))
        hidden = 0.5 * values * (1.0 + tanh)
        hid[c] = hidden.astype(jnp.bfloat16)
        turned[c] = hidden.T.astype(jnp.bfloat16)
        slope[c] = 0.5 * (1.0 + tanh) + 0.5 * values * (1.0 - tanh * tanh) * gelu_root * (
            1.0 + 3.0 * gelu_cubic * values * values
        )
        return carry

    lax.fori_loop(0, acc.shape[0], body, 0, unroll=4)
    send(0)
    send(1)
    need(2)
    down_terms(owner, down_rows, down_cols, turned, cot, out, lambda q: send(2, q))


def grad_pre_kernel(sides, need, send, owner, rows, cols, up_rows, up_cols, cot, w, slope, tok_turned, grad, out, acc):
    need(0)
    fetch = fetch_of(need, 1, sides)
    sum_blocks(acc, w.shape[0], sides, lambda k: cols[k], lambda k: dot(lanes(cot, rows[k]), w[k], 1, 1), fetch)
    need(2)

    def body(c, carry):
        grad[c] = (acc[c] * slope[c]).astype(jnp.bfloat16)
        return carry

    lax.fori_loop(0, acc.shape[0], body, 0, unroll=4)
    send(0)
    need(3)
    up_terms(owner, up_rows, up_cols, tok_turned, grad, out, lambda q: send(1, q))


def width_kernel(contract, sides, need, send, rows, cols, x, w, out, acc):
    need(0)
    fetch = fetch_of(need, 1, sides)
    sum_blocks(acc, w.shape[0], sides, lambda k: rows[k], lambda k: dot(x[cols[k]], w[k], 1, contract), fetch)
    for r in range(acc.shape[0]):
        out[:, r * BLK : (r + 1) * BLK] = acc[r].astype(jnp.bfloat16)


def tie(value, *others):
    return lax.optimization_barrier((value, others))[0]


def tensor_masks():
    masks = []
    mask = 1
    while mask < lax.axis_size("tensor"):
        masks.append(mask)
        mask *= 2
    return masks


def swap(value, mask):
    devices = lax.axis_size("tensor")
    return lax.ppermute(value, "tensor", [(i, i ^ mask) for i in range(devices)])


def gather_rows(value):
    for mask in reversed(tensor_masks()):
        value = jnp.concatenate([value, swap(value, mask)], axis=1)
    return value


def spread_sum(value):
    for mask in tensor_masks():
        half = value.shape[1] // 2
        other = swap(value[:, half:], mask)
        value = (value[:, :half].astype(jnp.float32) + other.astype(jnp.float32)).astype(jnp.bfloat16)
    return value


class RingSum:
    def __init__(self, parts, ahead, behind):
        self.parts, self.ahead, self.behind = parts, ahead, behind
        self.devices = parts.shape[0]
        self.done = 0
        self.run = (self.low(0), self.high((self.devices - 2) % self.devices))

    def low(self, q):
        return self.parts[q, :, : BLK // 2]

    def high(self, q):
        return self.parts[q, :, BLK // 2 :]

    def step(self):
        self.send()
        self.add()

    def send(self):
        a, b = (x.astype(jnp.bfloat16) for x in self.run)
        self.run = lax.ppermute(a, "dp", self.ahead), lax.ppermute(b, "dp", self.behind)

    def add(self, *after):
        self.done += 1
        last = self.done == self.devices - 1
        a, b = tie(self.run, *after) if after else self.run
        a = a.astype(jnp.float32) + self.low(self.done).astype(jnp.float32)
        q = self.done if last else self.devices - 2 - self.done
        b = b.astype(jnp.float32) + self.high(q).astype(jnp.float32)
        if not last:
            a, b = a.astype(jnp.bfloat16), b.astype(jnp.bfloat16)
        self.run = (a, b)

    def steps_left(self):
        return self.devices - 1 - self.done

    def total(self):
        return jnp.concatenate(self.run, axis=1)


def tables(rows, cols, owners):
    _, devices, slots = rows.shape
    live = devices * (slots // 2)
    counts = jnp.sum((cols >= 0).astype(jnp.int32), axis=2)
    earlier = owners[None, :] < owners[:, None]
    offset = jnp.sum(jnp.where(earlier[None], counts[:, None, :], 0), axis=2)
    within = jnp.arange(live, dtype=jnp.int32)[None, :, None] - offset[:, None, :]
    held = (within >= 0) & (within < counts[:, None, :])
    base = jnp.arange(devices, dtype=jnp.int32) * slots
    pick = jnp.sum(jnp.where(held, within + base[None, None, :], 0), axis=2)
    every = jnp.arange(devices * slots, dtype=jnp.int32)
    chosen = every[None, None, :] == pick[:, :, None]
    at = [jnp.sum(jnp.where(chosen, x.reshape(2, 1, devices * slots), 0), axis=2) for x in (rows, cols)]
    return pick, at[0], at[1]


def shards(tokens, cotangent, up_blocks, up_place, down_blocks, down_place):
    devices = lax.axis_size("dp")
    me = lax.axis_index("dp")
    slots = up_place.shape[2]
    mean = slots // 2
    live = devices * mean
    group_blocks = FF // BLK // lax.axis_size("tensor")
    row_count = tokens.shape[0] * lax.axis_size("tensor")
    model_width = tokens.shape[1]
    model_blocks = model_width // BLK

    order = ring_order(devices)
    place = {d: i for i, d in enumerate(order)}
    ahead, behind = ring_pairs(devices)
    nav = jnp.array(
        [
            [
                [order[(place[d] - j) % devices] for j in range(devices)],
                [order[(place[d] + j) % devices] for j in range(devices)],
                [order[(place[d] - 1 - j) % devices] for j in range(devices)],
            ]
            for d in range(devices)
        ],
        jnp.int32,
    )[me]
    from_ahead, from_behind, owner = nav[0], nav[1], nav[2]
    index = jnp.arange(devices, dtype=jnp.int32)
    up_slots = up_blocks.reshape(slots, BLK, BLK)
    down_slots = down_blocks.reshape(slots, BLK, BLK)
    codes = jnp.stack([up_place.reshape(1, slots), down_place.reshape(1, slots)])

    flops = 2 * live * row_count * BLK * BLK * WEIGHT
    block_bytes = live * BLK * BLK * 2
    side = row_count * BLK
    group_acc = pltpu.VMEM((group_blocks, row_count, BLK), jnp.float32)
    model_acc = pltpu.VMEM((model_blocks, row_count, BLK), jnp.float32)

    group_cube = (group_blocks, row_count, BLK)
    terms_shape = shape((devices, mean, BLK, BLK), jnp.bfloat16)

    def hidden_of(rows, cols, tok, cot, up):
        outs = [shape(group_cube, jnp.bfloat16), shape(group_cube, jnp.float32), terms_shape]
        return run(
            functools.partial(hidden_kernel, up.sides),
            [owner, rows[0], cols[0], rows[1], cols[1]],
            [Whole(tok), up, Whole(cot)],
            outs,
            [group_acc, pltpu.VMEM((group_blocks, BLK, row_count), jnp.bfloat16)],
            2 * flops,
            2 * block_bytes + side * (4 * model_blocks + 6 * group_blocks),
            [0, 0, devices],
        )

    def grad_pre_of(rows, cols, cot, down, slope, tok_turned):
        return run(
            functools.partial(grad_pre_kernel, down.sides),
            [owner, rows[1], cols[1], rows[0], cols[0]],
            [Whole(cot), down, Whole(slope), Whole(tok_turned)],
            [shape(group_cube, jnp.bfloat16), terms_shape],
            [group_acc],
            2 * flops,
            2 * block_bytes + side * (4 * model_blocks + 6 * group_blocks),
            [0, devices],
        )

    def width(contract, rows, cols, x, weights):
        outs = [shape((row_count, model_width), jnp.bfloat16)]
        nbytes = block_bytes + side * (2 * model_blocks + 2 * group_blocks)
        kernel = functools.partial(width_kernel, contract, weights.sides)
        return run(kernel, [rows, cols], [Whole(x), weights], outs, [model_acc], flops, nbytes)[0]

    if BLK % (PACK * devices) == 0 and slots <= BLK:
        here = me.reshape(1).astype(jnp.int32)
        messages = split_blocks(here, up_slots, down_slots, codes.reshape(2, slots), group_blocks, devices)
        parts = [messages[0]] * devices
        for step in range(1, devices):
            parts[step] = lax.ppermute(messages[step], "dp", [(i, i ^ step) for i in range(devices)])
        notes = jnp.stack([part[2 * slots, :4, :slots] for part in parts], axis=1).astype(jnp.int32)
        pick, rows, cols = tables(notes[:2], notes[2:], index ^ me)
        tok, cot = gather_rows(tie(jnp.stack([tokens, cotangent]), parts[1]))

        def onward(pair):
            return lax.ppermute(pair[0], "dp", ahead), lax.ppermute(pair[1], "dp", behind)

        tok_turned = tok.T

        up_ring = [pack_pieces(pick[0], parts, 0, slots, live)]
        down_ring = [pack_pieces(pick[1], parts, slots, slots, live)]
        for s in range(1, devices):
            up_ring.append(onward(tie(up_ring[-1], tok_turned) if s == devices // 2 else up_ring[-1]))
            down_ring.append(onward(down_ring[-1]))
        up, down = (Joined(*zip(*pairs, strict=True), (from_ahead, from_behind)) for pairs in (up_ring, down_ring))
    else:

        def everywhere(x, axis):
            return lax.all_gather(x, "dp", axis=axis, tiled=True)

        is_live = codes >= 0
        row_codes = jnp.where(is_live, codes // group_blocks, 0)
        col_codes = jnp.where(is_live, codes % group_blocks, -1)
        pick, rows, cols = tables(everywhere(row_codes, 1), everywhere(col_codes, 1), index)
        tok, cot = gather_rows(jnp.stack([tokens, cotangent]))
        tok_turned = tok.T
        up = Whole(jnp.take(everywhere(up_slots, 0), pick[0], axis=0))
        down = Whole(jnp.take(everywhere(down_slots, 0), pick[1], axis=0))

    hid, slope, terms = hidden_of(rows, cols, tok, cot, up)
    down_sum = RingSum(terms, ahead, behind)
    down_sum.send()
    grad_pre, terms = grad_pre_of(rows, cols, cot, down, slope, tok_turned)
    down_sum.add(grad_pre)
    up_sum = RingSum(terms, ahead, behind)
    up_sum.step()
    out_part = width(0, rows[1], cols[1], tie(hid, up_sum.run), down)
    up_sum.step()
    in_part = width(1, rows[0], cols[0], tie(grad_pre, out_part, up_sum.run), up)
    outputs, input_grads = spread_sum(jnp.stack([out_part, in_part]))
    while down_sum.steps_left():
        down_sum.step()
    while up_sum.steps_left():
        up_sum.step()

    scale = 1.0 / math.sqrt(devices * row_count)
    grads_shape = (1, 1, mean, BLK, BLK)
    up_grads = (up_sum.total() * scale).reshape(grads_shape)
    down_grads = (down_sum.total() * scale).reshape(grads_shape)
    return (outputs, input_grads, up_grads, down_grads)


def solution(mesh):
    return jax.shard_map(
        shards,
        mesh=mesh,
        in_specs=(
            P(("dp", "tensor"), None),
            P(("dp", "tensor"), None),
            P("dp", "tensor", None, None, None),
            P("dp", "tensor", None),
            P("dp", "tensor", None, None, None),
            P("dp", "tensor", None),
        ),
        out_specs=(
            P(("dp", "tensor"), None),
            P(("dp", "tensor"), None),
            P("dp", "tensor", None, None, None),
            P("dp", "tensor", None, None, None),
        ),
        check_vma=False,
    )
```

```python
import functools
import math

import jax
import jax.numpy as jnp
from jax import lax
from jax.experimental import pallas as pl
from jax.experimental.pallas import tpu as pltpu
from jax.sharding import PartitionSpec as P

FF = 16384
BLK = 128
PACK = 16
WEIGHT = 20
VMEM_LIMIT = 56 << 20

gelu_root = 0.7978845608028654
gelu_cubic = 0.044715

SMEM_SPEC = pl.BlockSpec(memory_space=pltpu.SMEM)
ANY_SPEC = pl.BlockSpec(memory_space=pl.ANY)


def ring_order(devices):
    evens = list(range(0, devices, 2))
    odds = list(range(1, devices, 2))
    return evens + odds[::-1]


def ring_pairs(devices):
    order = ring_order(devices)
    ahead = [(order[i], order[(i + 1) % devices]) for i in range(devices)]
    behind = [(b, a) for a, b in ahead]
    return ahead, behind


def shape(dims, dtype):
    return jax.ShapeDtypeStruct(tuple(dims), dtype)


def dot(a, b, ca, cb):
    return lax.dot_general(a, b, (((ca,), (cb,)), ((), ())), preferred_element_type=jnp.float32)


class Whole:
    sides = 1

    def __init__(self, array):
        self.arrays, self.tables = [array], []
        self.held = pltpu.VMEM(array.shape, array.dtype)

    def copies(self, tables, refs, held, sems):
        return [pltpu.make_async_copy(refs[0], held, sems.at[0])]


class Parts:
    def __init__(self, arrays, first, slots):
        self.arrays, self.tables, self.first, self.slots = list(arrays), [], first, slots
        self.held = pltpu.VMEM((len(arrays) * slots, *arrays[0].shape[1:]), arrays[0].dtype)

    def copies(self, tables, refs, held, sems):
        slots = self.slots
        return [
            pltpu.make_async_copy(ref.at[pl.ds(self.first, slots)], held.at[pl.ds(i * slots, slots)], sems.at[i])
            for i, ref in enumerate(refs)
        ]


class Joined:
    sides = 2

    def __init__(self, first, second, tables):
        self.arrays, self.tables = [*first, *second], list(tables)
        half = first[0].shape[0]
        self.held = pltpu.VMEM((2 * half, BLK, BLK), first[0].dtype)

    def copies(self, tables, refs, held, sems):
        half, piece, _ = refs[0].shape
        out = []
        for i, ref in enumerate(refs):
            side, j = divmod(i, len(refs) // 2)
            start = pl.multiple_of(tables[side][j] * piece, piece)
            to = held.at[pl.ds(side * half, half), pl.ds(start, piece), :]
            out.append(pltpu.make_async_copy(ref, to, sems.at[i]))
        return out


def run(kernel, small, items, outs, scratch=(), flops=0, nbytes=0, chunks=None):
    tables = [t for item in items for t in item.tables]
    arrays = [x for item in items for x in item.arrays]
    chunks = chunks or [0] * len(outs)

    def body(*refs):
        refs = list(refs)

        def take(n):
            taken = refs[:n]
            del refs[:n]
            return taken

        small_refs = take(len(small))
        table_refs = [take(len(item.tables)) for item in items]
        array_refs = [take(len(item.arrays)) for item in items]
        out_refs = take(len(outs))
        held_refs = take(len(items))
        result_refs = take(len(outs))
        scratch_refs = take(len(scratch))
        in_sems, out_sems = refs[: len(items)], refs[len(items) :]
        fetches = [
            item.copies(t, x, held, sems)
            for item, t, x, held, sems in zip(items, table_refs, array_refs, held_refs, in_sems, strict=True)
        ]
        for copies in fetches:
            for copy in copies[: len(copies) // 2 or 1]:
                copy.start()
        for copies in fetches:
            for copy in copies[len(copies) // 2 or 1 :]:
                copy.start()

        def need(*which, part=(0, 1)):
            for i in which:
                size = len(fetches[i]) // part[1]
                for copy in fetches[i][part[0] * size : (part[0] + 1) * size]:
                    copy.wait()

        sent = {}

        def send(i, q=None):
            result, out, sem = result_refs[i], out_refs[i], out_sems[i].at[q or 0]
            if q is not None:
                result, out = result.at[q], out.at[q]
            sent[i, q] = pltpu.make_async_copy(result, out, sem)
            sent[i, q].start()

        kernel(need, send, *small_refs, *held_refs, *result_refs, *scratch_refs)
        for i, count in enumerate(chunks):
            for q in range(count) if count else [None]:
                if (i, q) not in sent:
                    send(i, q)
        for copy in sent.values():
            copy.wait()

    return pl.pallas_call(
        body,
        out_shape=list(outs),
        in_specs=[SMEM_SPEC] * (len(small) + len(tables)) + [ANY_SPEC] * len(arrays),
        out_specs=[ANY_SPEC] * len(outs),
        scratch_shapes=[
            *(item.held for item in items),
            *(pltpu.VMEM(x.shape, x.dtype) for x in outs),
            *scratch,
            *(pltpu.SemaphoreType.DMA((len(item.arrays),)) for item in items),
            *(pltpu.SemaphoreType.DMA((max(1, count),)) for count in chunks),
        ],
        compiler_params=pltpu.CompilerParams(vmem_limit_bytes=VMEM_LIMIT),
        cost_estimate=pl.CostEstimate(flops=flops, bytes_accessed=nbytes, transcendentals=0),
    )(*small, *tables, *arrays)


def split_blocks(me, up, down, codes, group_blocks, devices):
    slots = up.shape[0]
    piece = BLK // devices

    def kernel(need, send, me_ref, codes_ref, up_ref, down_ref, *refs):
        *outs, note = refs
        need(0)
        code = codes_ref[...]
        live = code >= 0
        known = jnp.where(live, code, 0)
        note[...] = jnp.zeros_like(note)
        note[0:2, 0:slots] = lax.div(known, jnp.full_like(known, group_blocks)).astype(jnp.float32)
        note[2:4, 0:slots] = jnp.where(live, lax.rem(known, jnp.full_like(known, group_blocks)), -1).astype(jnp.float32)
        need(1, 2)
        for step, out in enumerate(outs):
            start = pl.multiple_of((me_ref[0] ^ step) * piece, piece)
            out[:slots] = up_ref[:, pl.ds(start, piece), :]
            out[slots : 2 * slots] = down_ref[:, pl.ds(start, piece), :]
            out[2 * slots] = note[...].astype(jnp.bfloat16)
            send(step)

    out = [shape((2 * slots + 1, piece, BLK), up.dtype)] * devices
    items = [Whole(codes), Whole(up), Whole(down)]
    return run(kernel, [me], items, out, [pltpu.VMEM((piece, BLK), jnp.float32)], nbytes=8 * up.size)


def pack_pieces(pick, parts, first, slots, live):
    piece = parts[0].shape[1]
    half = live // 2

    def kernel(need, send, pick_ref, held, *outs):
        need(0)
        for side, out in enumerate(outs):
            for k in range(half):
                out[k] = held[pick_ref[side * half + k]]
            send(side)

    out = [shape((half, piece, BLK), parts[0].dtype)] * 2
    nbytes = 3 * len(parts) * slots * piece * BLK
    return tuple(run(kernel, [pick], [Parts(parts, first, slots)], out, nbytes=nbytes))


def lanes(ref, block):
    return ref[:, pl.ds(pl.multiple_of(block * BLK, BLK), BLK)]


def sum_blocks(acc, live, sides, target, term, fetch):
    acc[...] = jnp.zeros_like(acc)
    count = live // sides
    for side in range(sides):
        fetch(side)
        for k in range(side * count, (side + 1) * count):
            acc[target(k)] += term(k)


def fetch_of(need, item, sides):
    return lambda side: need(item, part=(side, sides))


def down_terms(owner_ref, rows_ref, cols_ref, turned_ref, cot_ref, out_ref, send):
    devices, mean = out_ref.shape[:2]
    for q in range(devices):
        base = owner_ref[q] * mean
        for j in range(mean):
            row, col = rows_ref[base + j], cols_ref[base + j]
            out_ref[q, j] = dot(turned_ref[col], lanes(cot_ref, row), 1, 0).astype(jnp.bfloat16)
        send(q)


def up_terms(owner_ref, rows_ref, cols_ref, turned_ref, grad_ref, out_ref, send):
    devices, mean = out_ref.shape[:2]
    for q in range(devices):
        base = owner_ref[q] * mean
        for j in range(mean):
            row, col = rows_ref[base + j], cols_ref[base + j]
            turned = turned_ref[pl.ds(pl.multiple_of(row * BLK, BLK), BLK), :]
            out_ref[q, j] = dot(turned, grad_ref[col], 1, 0).astype(jnp.bfloat16)
        send(q)


def hidden_kernel(sides, need, send, owner, rows, cols, down_rows, down_cols, tok, w, cot, hid, slope, out, acc, turned):
    need(0)
    fetch = fetch_of(need, 1, sides)
    sum_blocks(acc, w.shape[0], sides, lambda k: cols[k], lambda k: dot(lanes(tok, rows[k]), w[k], 1, 0), fetch)

    def body(c, carry):
        values = acc[c]
        tanh = jnp.tanh(gelu_root * (values + gelu_cubic * values * values * values))
        hidden = 0.5 * values * (1.0 + tanh)
        hid[c] = hidden.astype(jnp.bfloat16)
        turned[c] = hidden.T.astype(jnp.bfloat16)
        slope[c] = 0.5 * (1.0 + tanh) + 0.5 * values * (1.0 - tanh * tanh) * gelu_root * (
            1.0 + 3.0 * gelu_cubic * values * values
        )
        return carry

    lax.fori_loop(0, acc.shape[0], body, 0, unroll=8)
    send(0)
    send(1)
    need(2)
    down_terms(owner, down_rows, down_cols, turned, cot, out, lambda q: send(2, q))


def grad_pre_kernel(sides, need, send, owner, rows, cols, up_rows, up_cols, cot, w, slope, tok_turned, grad, out, acc):
    need(0)
    fetch = fetch_of(need, 1, sides)
    sum_blocks(acc, w.shape[0], sides, lambda k: cols[k], lambda k: dot(lanes(cot, rows[k]), w[k], 1, 1), fetch)
    need(2)

    def body(c, carry):
        grad[c] = (acc[c] * slope[c]).astype(jnp.bfloat16)
        return carry

    lax.fori_loop(0, acc.shape[0], body, 0, unroll=8)
    send(0)
    need(3)
    up_terms(owner, up_rows, up_cols, tok_turned, grad, out, lambda q: send(1, q))


def width_kernel(contract, sides, need, send, rows, cols, x, w, out, acc):
    need(0)
    fetch = fetch_of(need, 1, sides)
    sum_blocks(acc, w.shape[0], sides, lambda k: rows[k], lambda k: dot(x[cols[k]], w[k], 1, contract), fetch)
    for r in range(acc.shape[0]):
        out[:, r * BLK : (r + 1) * BLK] = acc[r].astype(jnp.bfloat16)


def tie(value, *others):
    return lax.optimization_barrier((value, others))[0]


def tensor_masks():
    masks = []
    mask = 1
    while mask < lax.axis_size("tensor"):
        masks.append(mask)
        mask *= 2
    return masks


def swap(value, mask):
    devices = lax.axis_size("tensor")
    return lax.ppermute(value, "tensor", [(i, i ^ mask) for i in range(devices)])


def gather_rows(value):
    for mask in reversed(tensor_masks()):
        value = jnp.concatenate([value, swap(value, mask)], axis=1)
    return value


def spread_sum(value):
    for mask in tensor_masks():
        half = value.shape[1] // 2
        other = swap(value[:, half:], mask)
        value = (value[:, :half].astype(jnp.float32) + other.astype(jnp.float32)).astype(jnp.bfloat16)
    return value


class RingSum:
    def __init__(self, parts, ahead, behind):
        self.parts, self.ahead, self.behind = parts, ahead, behind
        self.devices = parts.shape[0]
        self.done = 0
        self.run = (self.low(0), self.high((self.devices - 2) % self.devices))

    def low(self, q):
        return self.parts[q, :, : BLK // 2]

    def high(self, q):
        return self.parts[q, :, BLK // 2 :]

    def step(self):
        self.send()
        self.add()

    def send(self):
        a, b = (x.astype(jnp.bfloat16) for x in self.run)
        self.run = lax.ppermute(a, "dp", self.ahead), lax.ppermute(b, "dp", self.behind)

    def add(self, *after):
        self.done += 1
        last = self.done == self.devices - 1
        a, b = tie(self.run, *after) if after else self.run
        a = a.astype(jnp.float32) + self.low(self.done).astype(jnp.float32)
        q = self.done if last else self.devices - 2 - self.done
        b = b.astype(jnp.float32) + self.high(q).astype(jnp.float32)
        if not last:
            a, b = a.astype(jnp.bfloat16), b.astype(jnp.bfloat16)
        self.run = (a, b)

    def steps_left(self):
        return self.devices - 1 - self.done

    def total(self):
        return jnp.concatenate(self.run, axis=1)


def tables(rows, cols, owners):
    _, devices, slots = rows.shape
    live = devices * (slots // 2)
    counts = jnp.sum((cols >= 0).astype(jnp.int32), axis=2)
    earlier = owners[None, :] < owners[:, None]
    offset = jnp.sum(jnp.where(earlier[None], counts[:, None, :], 0), axis=2)
    within = jnp.arange(live, dtype=jnp.int32)[None, :, None] - offset[:, None, :]
    held = (within >= 0) & (within < counts[:, None, :])
    base = jnp.arange(devices, dtype=jnp.int32) * slots
    pick = jnp.sum(jnp.where(held, within + base[None, None, :], 0), axis=2)
    every = jnp.arange(devices * slots, dtype=jnp.int32)
    chosen = every[None, None, :] == pick[:, :, None]
    at = [jnp.sum(jnp.where(chosen, x.reshape(2, 1, devices * slots), 0), axis=2) for x in (rows, cols)]
    return pick, at[0], at[1]


def shards(tokens, cotangent, up_blocks, up_place, down_blocks, down_place):
    devices = lax.axis_size("dp")
    me = lax.axis_index("dp")
    slots = up_place.shape[2]
    mean = slots // 2
    live = devices * mean
    group_blocks = FF // BLK // lax.axis_size("tensor")
    row_count = tokens.shape[0] * lax.axis_size("tensor")
    model_width = tokens.shape[1]
    model_blocks = model_width // BLK

    order = ring_order(devices)
    place = {d: i for i, d in enumerate(order)}
    ahead, behind = ring_pairs(devices)
    nav = jnp.array(
        [
            [
                [order[(place[d] - j) % devices] for j in range(devices)],
                [order[(place[d] + j) % devices] for j in range(devices)],
                [order[(place[d] - 1 - j) % devices] for j in range(devices)],
            ]
            for d in range(devices)
        ],
        jnp.int32,
    )[me]
    from_ahead, from_behind, owner = nav[0], nav[1], nav[2]
    index = jnp.arange(devices, dtype=jnp.int32)
    up_slots = up_blocks.reshape(slots, BLK, BLK)
    down_slots = down_blocks.reshape(slots, BLK, BLK)
    codes = jnp.stack([up_place.reshape(1, slots), down_place.reshape(1, slots)])

    flops = 2 * live * row_count * BLK * BLK * WEIGHT
    block_bytes = live * BLK * BLK * 2
    side = row_count * BLK
    group_acc = pltpu.VMEM((group_blocks, row_count, BLK), jnp.float32)
    model_acc = pltpu.VMEM((model_blocks, row_count, BLK), jnp.float32)

    group_cube = (group_blocks, row_count, BLK)
    terms_shape = shape((devices, mean, BLK, BLK), jnp.bfloat16)

    def hidden_of(rows, cols, tok, cot, up):
        outs = [shape(group_cube, jnp.bfloat16), shape(group_cube, jnp.float32), terms_shape]
        return run(
            functools.partial(hidden_kernel, up.sides),
            [owner, rows[0], cols[0], rows[1], cols[1]],
            [Whole(tok), up, Whole(cot)],
            outs,
            [group_acc, pltpu.VMEM((group_blocks, BLK, row_count), jnp.bfloat16)],
            2 * flops,
            2 * block_bytes + side * (4 * model_blocks + 6 * group_blocks),
            [0, 0, devices],
        )

    def grad_pre_of(rows, cols, cot, down, slope, tok_turned):
        return run(
            functools.partial(grad_pre_kernel, down.sides),
            [owner, rows[1], cols[1], rows[0], cols[0]],
            [Whole(cot), down, Whole(slope), Whole(tok_turned)],
            [shape(group_cube, jnp.bfloat16), terms_shape],
            [group_acc],
            2 * flops,
            2 * block_bytes + side * (4 * model_blocks + 6 * group_blocks),
            [0, devices],
        )

    def width(contract, rows, cols, x, weights):
        outs = [shape((row_count, model_width), jnp.bfloat16)]
        nbytes = block_bytes + side * (2 * model_blocks + 2 * group_blocks)
        kernel = functools.partial(width_kernel, contract, weights.sides)
        return run(kernel, [rows, cols], [Whole(x), weights], outs, [model_acc], flops, nbytes)[0]

    if BLK % (PACK * devices) == 0 and slots <= BLK:
        here = me.reshape(1).astype(jnp.int32)
        messages = split_blocks(here, up_slots, down_slots, codes.reshape(2, slots), group_blocks, devices)
        parts = [messages[0]] * devices
        for step in range(1, devices):
            parts[step] = lax.ppermute(messages[step], "dp", [(i, i ^ step) for i in range(devices)])
        notes = jnp.stack([part[2 * slots, :4, :slots] for part in parts], axis=1).astype(jnp.int32)
        pick, rows, cols = tables(notes[:2], notes[2:], index ^ me)
        tok, cot = gather_rows(tie(jnp.stack([tokens, cotangent]), parts[1]))

        def onward(pair):
            return lax.ppermute(pair[0], "dp", ahead), lax.ppermute(pair[1], "dp", behind)

        tok_turned = tok.T

        up_ring = [pack_pieces(pick[0], parts, 0, slots, live)]
        down_ring = [pack_pieces(pick[1], parts, slots, slots, live)]
        for s in range(1, devices):
            up_ring.append(onward(tie(up_ring[-1], tok_turned) if s == devices // 2 else up_ring[-1]))
            down_ring.append(onward(down_ring[-1]))
        up, down = (Joined(*zip(*pairs, strict=True), (from_ahead, from_behind)) for pairs in (up_ring, down_ring))
    else:

        def everywhere(x, axis):
            return lax.all_gather(x, "dp", axis=axis, tiled=True)

        is_live = codes >= 0
        row_codes = jnp.where(is_live, codes // group_blocks, 0)
        col_codes = jnp.where(is_live, codes % group_blocks, -1)
        pick, rows, cols = tables(everywhere(row_codes, 1), everywhere(col_codes, 1), index)
        tok, cot = gather_rows(jnp.stack([tokens, cotangent]))
        tok_turned = tok.T
        up = Whole(jnp.take(everywhere(up_slots, 0), pick[0], axis=0))
        down = Whole(jnp.take(everywhere(down_slots, 0), pick[1], axis=0))

    hid, slope, terms = hidden_of(rows, cols, tok, cot, up)
    down_sum = RingSum(terms, ahead, behind)
    down_sum.send()
    grad_pre, terms = grad_pre_of(rows, cols, cot, down, slope, tok_turned)
    down_sum.add(grad_pre)
    up_sum = RingSum(terms, ahead, behind)
    up_sum.step()
    out_part = width(0, rows[1], cols[1], tie(hid, up_sum.run), down)
    up_sum.step()
    in_part = width(1, rows[0], cols[0], tie(grad_pre, out_part, up_sum.run), up)
    outputs, input_grads = spread_sum(jnp.stack([out_part, in_part]))
    while down_sum.steps_left():
        down_sum.step()
    while up_sum.steps_left():
        up_sum.step()

    scale = 1.0 / math.sqrt(devices * row_count)
    grads_shape = (1, 1, mean, BLK, BLK)
    up_grads = (up_sum.total() * scale).reshape(grads_shape)
    down_grads = (down_sum.total() * scale).reshape(grads_shape)
    return (outputs, input_grads, up_grads, down_grads)


def solution(mesh):
    return jax.shard_map(
        shards,
        mesh=mesh,
        in_specs=(
            P(("dp", "tensor"), None),
            P(("dp", "tensor"), None),
            P("dp", "tensor", None, None, None),
            P("dp", "tensor", None),
            P("dp", "tensor", None, None, None),
            P("dp", "tensor", None),
        ),
        out_specs=(
            P(("dp", "tensor"), None),
            P(("dp", "tensor"), None),
            P("dp", "tensor", None, None, None),
            P("dp", "tensor", None, None, None),
        ),
        check_vma=False,
    )
```
